32 devices in a mesh: tm: 4 (over z), tile: 2 (over y), clip: 4 (over x, core).
Axes of the slice: x: 2, y: 2, z: 4, core: 2. Of those that a mesh axis runs over, the one named last changes fastest.
Arguments:
- latents: bfloat16 [32, 16, 128, 256], P(('clip', 'tm'), 'tile'), parts along dimension 0, may hold values from -40 to 40
- norm1_gain: float32 [256], replicated, may hold values from 0.1 to 1.9
- conv1_weight: bfloat16 [27, 256, 256], P(None, None, ('tm', 'tile')), may hold values from -0.078125 to 0.078125
- conv1_bias: float32 [256], replicated, may hold values from -3 to 3
- norm2_gain: float32 [256], replicated, may hold values from 0.1 to 1.9
- conv2_weight: bfloat16 [27, 256, 256], P(None, None, ('tm', 'tile')), may hold values from -0.078125 to 0.078125
- conv2_bias: float32 [256], replicated, may hold values from -3 to 3
Outputs:
- decoded: bfloat16 [32, 16, 128, 256], P(('clip', 'tm'), 'tile'), parts along dimension 0
The draws below stay inside these ranges and needn't reach their ends.
There are 4 independent parts, one for each index of `clip`. The reference program is written for one: setup_inputs(seed, part) draws one part's arguments, and reference() takes and returns one part's arrays. A program takes and returns all parts, laid end to end along the dimension named above; an argument that names none is the same for every part. Nothing has to cross between parts.
All inputs are finite; a program needn't handle non-finite values.
Results may differ from the reference program's by a relative error of at most 0.003.
Values may be sent and summed in bfloat16 or wider, within the bound.
No kernel may reach another device: no remote copies, remote signals or barrier semaphores. Data moves between devices by JAX's collectives and lax.ppermute only.
A program may use at most 64 MiB of HBM per device.

```python
import math
import jax
import jax.numpy as jnp
from jax import lax

C = 256
GROUPS = 32
COLS = 128
FRAMES = 8
HEIGHT = 16


def draw_latents(key, part):
    base = jax.random.fold_in(key, 11)
    key_one = jax.random.fold_in(base, 0)
    key_two = jax.random.fold_in(base, 1)
    key_three = jax.random.fold_in(base, 2)
    key_five = jax.random.fold_in(base, 4)
    key_six = jax.random.fold_in(base, 5)
    key_seven = jax.random.fold_in(base, 6)
    shape = (FRAMES, HEIGHT, COLS, C)
    chan_scale = jnp.exp(jax.random.uniform(key_two, (C,), jnp.float32, math.log(0.3), math.log(3.0)))
    row_pos = jnp.arange(HEIGHT, dtype=jnp.float32) / max(HEIGHT - 1, 1)
    row_scale = jnp.exp(math.log(0.5) + math.log(3.0) * row_pos)[None, :, None, None]
    rough = jax.random.uniform(key_three, shape, jnp.float32, 0.5, 1.5)
    row_angle = jnp.arange(HEIGHT, dtype=jnp.float32) * (2.0 * math.pi / HEIGHT)
    col_angle = jnp.arange(COLS, dtype=jnp.float32) * (2.0 * math.pi / COLS)
    phases = jax.random.uniform(key_five, (FRAMES, 3, 2), jnp.float32, 0.0, 2.0 * math.pi)
    amplitudes = jax.random.uniform(key_six, (FRAMES, 3), jnp.float32, 0.6, 1.2)
    smooth = jnp.zeros((FRAMES, HEIGHT, COLS), jnp.float32)
    for index, pair in enumerate(((1.0, 1.0), (2.0, 1.0), (1.0, 2.0))):
        row_wave = jnp.cos(pair[0] * row_angle[None, :, None] + phases[:, index, 0][:, None, None])
        col_wave = jnp.cos(pair[1] * col_angle[None, None, :] + phases[:, index, 1][:, None, None])
        smooth = smooth + amplitudes[:, index][:, None, None] * row_wave * col_wave
    trend = jnp.clip(jax.random.normal(key_seven, (FRAMES, 1, 1, C), jnp.float32), -2.0, 2.0) * (2.0 * row_pos - 1.0)[None, :, None, None]
    noise = jnp.clip(jax.random.normal(key_one, shape, jnp.float32), -4.0, 4.0)
    values = noise * chan_scale * row_scale * rough + (trend + smooth[:, :, :, None]) * chan_scale
    values = jnp.clip(values, -39.0, 39.0)
    return values.astype(jnp.bfloat16)


def block_scale(stream_key, shape, cuts, low, largest):
    loudness = 1.0
    for axis_at, blocks in cuts:
        draws = jax.random.uniform(jax.random.fold_in(jax.random.fold_in(stream_key, 6), axis_at), (blocks,), jnp.float32, low / len(cuts), largest / len(cuts))
        loudness = loudness * jnp.repeat(jnp.exp(draws), shape[axis_at] // blocks).reshape((-1,) + (1,) * (len(shape) - 1 - axis_at))
    return loudness


def bell_draw(stream_key, dims, spread, limit, cuts=(), kind=jnp.bfloat16):
    drawn = jax.random.normal(stream_key, dims, jnp.float32) * spread
    if len(cuts) > 0:
        drawn = block_scale(stream_key, dims, cuts, -0.22, 0.18) * drawn
    return jnp.clip(drawn, min=-limit, max=limit).astype(kind)


def setup_inputs(seed: int = 0, part: int = 0) -> dict:
    key_list = jax.random.split(jax.random.key(seed), 8)
    own_keys = jax.random.split(jax.random.fold_in(key_list[7], part), 8)
    latents = draw_latents(jax.random.fold_in(jax.random.fold_in(key_list[7], part), 71), part)
    norm1_gain = jnp.clip(1.0 + 0.18 * jax.random.normal(key_list[1], (C,), jnp.float32), 0.1, 1.9)
    conv1_weight = bell_draw(key_list[2], (27, C, C), (27 * C) ** -0.5, 0.078125, ((2, 8),))
    conv1_bias = bell_draw(key_list[3], (C,), 0.5, 3.0, (), jnp.float32)
    norm2_gain = jnp.clip(1.0 + 0.18 * jax.random.normal(key_list[4], (C,), jnp.float32), 0.1, 1.9)
    conv2_weight = bell_draw(key_list[5], (27, C, C), (27 * C) ** -0.5, 0.078125, ((2, 8),))
    conv2_bias = bell_draw(key_list[6], (C,), 0.5, 3.0, (), jnp.float32)
    return {"latents": latents, "norm1_gain": norm1_gain, "conv1_weight": conv1_weight, "conv1_bias": conv1_bias, "norm2_gain": norm2_gain, "conv2_weight": conv2_weight, "conv2_bias": conv2_bias}


epsilon = 1e-06

def normalize(inputs_f, gain_vec):
    frames, height, columns, channels = inputs_f.shape
    grouped = inputs_f.reshape(frames, height, columns, GROUPS, channels // GROUPS)
    group_mean = lax.optimization_barrier(jnp.mean(grouped, axis=(1, 2, 4), keepdims=True))
    centered = grouped - group_mean
    group_var = lax.optimization_barrier(jnp.mean(centered * centered, axis=(1, 2, 4), keepdims=True))
    normed = (centered * lax.rsqrt(group_var + epsilon)).reshape(inputs_f.shape) * gain_vec
    return jax.nn.silu(normed).astype(jnp.bfloat16)

def convolve(activated, weight_full, bias_vec):
    frames, height, columns, channels = activated.shape
    padded = jnp.pad(activated, ((2, 0), (1, 1), (1, 1), (0, 0)))
    widened = jnp.concatenate([padded[:, :, shift_col:shift_col + columns] for shift_col in range(3)], axis=-1)
    kernel = weight_full.reshape(3, 3, 3 * channels, channels)
    summed = jnp.zeros((frames * height * columns, channels), jnp.float32) + bias_vec
    for frame_off in range(3):
        for row_off in range(3):
            block_rows = widened[frame_off:frame_off + frames, row_off:row_off + height].reshape(-1, 3 * channels)
            summed = summed + jnp.dot(block_rows.astype(jnp.float32), kernel[frame_off, row_off].astype(jnp.float32))
    return summed.reshape(frames, height, columns, channels)

def reference(latents, norm1_gain, conv1_weight, conv1_bias, norm2_gain, conv2_weight, conv2_bias):
    inputs_f = latents.astype(jnp.float32)
    hidden = convolve(normalize(inputs_f, norm1_gain), conv1_weight, conv1_bias).astype(jnp.bfloat16)
    second = convolve(normalize(hidden.astype(jnp.float32), norm2_gain), conv2_weight, conv2_bias)
    return (inputs_f + second).astype(jnp.bfloat16)
```

```python
import functools

import jax
import jax.numpy as jnp
from jax import lax
from jax.experimental import pallas as pl
from jax.experimental.pallas import tpu as pltpu
from jax.sharding import PartitionSpec as P

GROUPS = 32
TAPS = 27
epsilon = 1e-06
F32 = jnp.float32
BF16 = jnp.bfloat16
NT = (((1,), (1,)), ((), ()))


def upward(value, axis, steps=1):
    count = lax.axis_size(axis)
    first, last = (max(0, -steps), min(count, count - steps))
    return lax.ppermute(value, axis, [(source, source + steps) for source in range(first, last)])


def cyclic(value, axis, steps):
    count = lax.axis_size(axis)
    return lax.ppermute(value, axis, [(i, (i + steps) % count) for i in range(count)])


def swap(value, axis, bit):
    count = lax.axis_size(axis)
    return lax.ppermute(value, axis, [(i, i ^ bit) for i in range(count)])


def edge_rows(block):
    tiles = lax.axis_size("tile")
    if tiles == 2:
        mine = jnp.where(lax.axis_index("tile") == 0, block[:, -1:], block[:, :1])
        own = swap(mine, "tile", 1)
        blocks = lax.axis_size("tm")
        pairs = [(t * 2 + y, (t + 1) * 2 + 1 - y) for t in range(blocks - 1) for y in range(2)]
        before = lax.ppermute(mine, ("tm", "tile"), pairs)
        return own, own, before, before
    low = upward(block[:, -1:], "tile", 1)
    high = upward(block[:, :1], "tile", -1)
    return low, high, upward(low, "tm"), upward(high, "tm")


def share_stats(stats):
    if lax.axis_size("tile") == 2:
        both = jnp.stack([stats, swap(stats, "tile", 1)])
    else:
        both = lax.all_gather(stats, "tile", axis=0)
    return both, upward(both, "tm")


def piece_kernel(w_ref, o_ref, held, sem):
    clip = lax.axis_index("clip")
    half, core = clip // 2, clip % 2
    count = held.shape[0]
    copy = pltpu.make_async_copy(w_ref.at[pl.ds(half * count, count)], held, sem)
    copy.start()
    rows, shard = o_ref.shape[0], held.shape[2]
    row = lax.broadcasted_iota(jnp.int32, (rows, shard), 0) + rows * core
    col = lax.broadcasted_iota(jnp.int32, (rows, shard), 1)
    pick = jnp.where(row == col, 1.0, 0.0).astype(BF16)
    copy.wait()
    for j in range(count):
        part = lax.dot_general(pick, held[j], NT, preferred_element_type=F32)
        o_ref[:, j * 128 : (j + 1) * 128] = part.astype(BF16)


def own_piece(shard):
    taps, depth, outs = shard.shape
    units = taps * depth // 128
    return pl.pallas_call(
        piece_kernel,
        out_shape=jax.ShapeDtypeStruct((outs // 2, taps * depth // 2), BF16),
        in_specs=[pl.BlockSpec(memory_space=pl.ANY)],
        out_specs=pl.BlockSpec(memory_space=pltpu.VMEM),
        scratch_shapes=[pltpu.VMEM((units // 2, 128, outs), BF16), pltpu.SemaphoreType.DMA],
        name="piece",
    )(shard.reshape(units, 128, outs))


HELD = (
    ((0, 0, 0), (1, 0, 0), (2, 0, 0), (3, 0, 0)),
    ((0, 0, 1), (1, 0, 1), (2, 0, 1), (3, 0, 1)),
    ((0, 1, 0), (1, 1, 0), (2, 1, 0), (3, 1, 0)),
    ((0, 1, 1), (1, 1, 1)),
    ((2, 1, 1), (3, 1, 1)),
)


def gather_weights(shard):
    tm, tile, clip = (lax.axis_size(a) for a in ("tm", "tile", "clip"))
    if (tm, tile, clip) != (4, 2, 4):
        whole = lax.all_gather(shard, ("tm", "tile"), axis=2, tiled=True)
        return [whole.reshape(-1, whole.shape[2]).T]
    piece = own_piece(shard)
    held = jnp.stack([piece] + [cyclic(piece, "tm", steps) for steps in (1, 2, 3)])
    across = swap(held, "clip", 2)
    beside = swap(held, "tile", 1)
    corner_a = swap(beside[:2], "clip", 2)
    corner_b = swap(across[2:], "tile", 1)
    arrays = [held, across, beside, corner_a, corner_b]
    return arrays + [swap(a, "clip", 1) for a in arrays]


def channel_stats(rows):
    mean = jnp.sum(rows, axis=0, keepdims=True) / rows.shape[0]
    centered = rows - mean
    return mean, jnp.sum(centered * centered, axis=0, keepdims=True)


def stats_kernel(x_ref, s_ref):
    frames, rows, columns, channels = x_ref.shape
    for f in range(frames):
        mean, spread = channel_stats(x_ref[f].astype(F32).reshape(rows * columns, channels))
        s_ref[f : f + 1] = mean
        s_ref[frames + f : frames + f + 1] = spread


def stats_of(block):
    frames, _, _, channels = block.shape
    return pl.pallas_call(
        stats_kernel,
        out_shape=jax.ShapeDtypeStruct((2 * frames, channels), F32),
        in_specs=[pl.BlockSpec(memory_space=pltpu.VMEM)],
        out_specs=pl.BlockSpec(memory_space=pltpu.VMEM),
        name="stats",
    )(block)


def norm_terms(stats, gain, cells):
    tiles, twice, channels = stats.shape
    frames = twice // 2
    width = channels // GROUPS
    a = lax.broadcasted_iota(jnp.int32, (channels, channels), 0) // width
    b = lax.broadcasted_iota(jnp.int32, (channels, channels), 1) // width
    same = jnp.where(a == b, 1.0, 0.0).astype(F32)
    pool = functools.partial(jnp.dot, precision=lax.Precision.HIGHEST, preferred_element_type=F32)
    mean = pool(jnp.sum(stats[:, :frames], axis=0), same) / (tiles * width)
    off = stats[:, :frames] - mean[None]
    spread = jnp.sum(stats[:, frames:] + cells * (off * off), axis=0)
    var = pool(spread, same) / (tiles * width * cells)
    return mean, lax.rsqrt(var + epsilon) * gain


def conv_kernel(n_weights, residual, *refs):
    own, prev, low_o, high_o, low_p, high_p, st_o, st_p, gain, bias = refs[:10]
    weights = refs[10 : 10 + n_weights]
    if residual:
        extra, out = refs[10 + n_weights : 12 + n_weights]
        wide, full, sems = refs[12 + n_weights :]
    else:
        out, stats_out = refs[10 + n_weights : 12 + n_weights]
        wide, full, sems = refs[12 + n_weights :]
    frames, rows, columns, channels = own.shape
    span = 3 * channels

    copies = []
    if n_weights == 1:
        copies.append(pltpu.make_async_copy(weights[0], full, sems.at[0]))
    else:
        tm, tile, clip = (lax.axis_index(a) for a in ("tm", "tile", "clip"))
        half, core = clip // 2, clip % 2
        _, high, deep = weights[0].shape
        for side in range(2):
            for group, names in enumerate(HELD):
                for at, (back, dy, dx) in enumerate(names):
                    block = (lax.rem(tm + 4 - back, 4) * 2 + (tile ^ dy)) * 2 + (core ^ side)
                    place = full.at[
                        pl.ds(pl.multiple_of(block * high, high), high),
                        pl.ds(pl.multiple_of((half ^ dx) * deep, 128), deep),
                    ]
                    source = weights[side * len(HELD) + group].at[at]
                    copies.append(pltpu.make_async_copy(source, place, sems.at[len(copies)]))
    for copy in copies:
        copy.start()

    cells = float(rows * columns)
    here = norm_terms(st_o[...], gain[...], cells)
    before = norm_terms(st_p[...], gain[...], cells)
    first_tile = lax.axis_index("tile") == 0
    last_tile = lax.axis_index("tile") == lax.axis_size("tile") - 1
    start = lax.axis_index("tm") == 0
    column = lax.broadcasted_iota(jnp.int32, (columns, channels), 0)

    def put(slot, row, raw, mean, scale, empty):
        half_y = (raw.astype(F32) - mean) * (0.5 * scale)
        y = half_y * (1.0 + jnp.tanh(half_y))
        if empty is not None:
            y = jnp.where(empty, 0.0, y)
        left = jnp.where(column == 0, 0.0, pltpu.roll(y, 1, 0))
        right = jnp.where(column == columns - 1, 0.0, pltpu.roll(y, columns - 1, 0))
        wide[slot, row, :, :channels] = left.astype(BF16)
        wide[slot, row, :, channels : 2 * channels] = y.astype(BF16)
        wide[slot, row, :, 2 * channels :] = right.astype(BF16)

    for f in range(2):
        mean, scale = here[0][f : f + 1], here[1][f : f + 1]

        def body(r, carry, f=f, mean=mean, scale=scale):
            put(2 + f, r + 1, own[f, r], mean, scale, None)
            return carry

        lax.fori_loop(0, rows, body, 0)
        put(2 + f, 0, low_o[f, 0], mean, scale, first_tile)
        put(2 + f, rows + 1, high_o[f, 0], mean, scale, last_tile)
    for f in range(2):
        mean, scale = before[0][f : f + 1], before[1][f : f + 1]

        def body(r, carry, f=f, mean=mean, scale=scale):
            put(f, r + 1, prev[f, r], mean, scale, start)
            return carry

        lax.fori_loop(0, rows, body, 0)
        put(f, 0, low_p[f, 0], mean, scale, start | first_tile)
        put(f, rows + 1, high_p[f, 0], mean, scale, start | last_tile)

    for copy in copies:
        copy.wait()

    def frame(f, carry):
        total = jnp.broadcast_to(bias[...], (rows * columns, channels))
        for df in range(3):
            for dh in range(3):
                left = wide[f + df, dh : dh + rows].reshape(rows * columns, span)
                at = (3 * df + dh) * span
                total = total + lax.dot_general(
                    left, full[:, at : at + span], NT, preferred_element_type=F32
                )
        if residual:
            total = total + extra[f].astype(F32).reshape(rows * columns, channels)
        done = total.astype(BF16)
        out[f] = done.reshape(rows, columns, channels)
        if not residual:
            mean, spread = channel_stats(done.astype(F32))
            stats_out[pl.ds(f, 1)] = mean
            stats_out[pl.ds(frames + f, 1)] = spread
        return carry

    lax.fori_loop(0, frames, frame, 0)


def conv(own, prev, edges, stats, gain, bias, weights, extra=None):
    frames, rows, columns, channels = own.shape
    vmem = pl.BlockSpec(memory_space=pltpu.VMEM)
    shapes = [jax.ShapeDtypeStruct(own.shape, BF16)]
    args = [own, prev, *edges, *stats, gain[None], bias[None], *weights]
    specs = [vmem] * 10 + [pl.BlockSpec(memory_space=pl.ANY)] * len(weights)
    if extra is None:
        shapes.append(jax.ShapeDtypeStruct((2 * frames, channels), F32))
    else:
        args.append(extra)
        specs.append(vmem)
    flops = 2 * frames * rows * columns * channels * channels * TAPS
    return pl.pallas_call(
        functools.partial(conv_kernel, len(weights), extra is not None),
        out_shape=shapes,
        in_specs=specs,
        out_specs=[vmem] * len(shapes),
        scratch_shapes=[
            pltpu.VMEM((4, rows + 2, columns, 3 * channels), BF16),
            pltpu.VMEM((channels, TAPS * channels), BF16),
            pltpu.SemaphoreType.DMA((32,)),
        ],
        cost_estimate=pl.CostEstimate(flops=flops, bytes_accessed=9 << 20, transcendentals=1 << 20),
        name="conv",
    )(*args)


def shards(latents, norm1_gain, conv1_weight, conv1_bias, norm2_gain, conv2_weight, conv2_bias):
    weights1 = gather_weights(conv1_weight)
    prev = upward(latents, "tm")
    edges = edge_rows(latents)
    stats = share_stats(stats_of(latents))
    hidden, sums = conv(latents, prev, edges, stats, norm1_gain, conv1_bias, weights1)
    weights2 = gather_weights(conv2_weight)
    prev = upward(hidden, "tm")
    edges = edge_rows(hidden)
    stats = share_stats(sums)
    return conv(hidden, prev, edges, stats, norm2_gain, conv2_bias, weights2, latents)[0]


def solution(mesh):
    placed = (
        P(("clip", "tm"), "tile", None, None),
        P(),
        P(None, None, ("tm", "tile")),
        P(),
        P(),
        P(None, None, ("tm", "tile")),
        P(),
    )
    return jax.shard_map(
        shards,
        mesh=mesh,
        in_specs=placed,
        out_specs=P(("clip", "tm"), "tile", None, None),
        check_vma=False,
    )
```

```python
import functools

import jax
import jax.numpy as jnp
from jax import lax
from jax.experimental import pallas as pl
from jax.experimental.pallas import tpu as pltpu
from jax.sharding import PartitionSpec as P

GROUPS = 32
TAPS = 27
epsilon = 1e-06
F32 = jnp.float32
BF16 = jnp.bfloat16
NT = (((1,), (1,)), ((), ()))


def upward(value, axis, steps=1):
    count = lax.axis_size(axis)
    first, last = (max(0, -steps), min(count, count - steps))
    return lax.ppermute(value, axis, [(source, source + steps) for source in range(first, last)])


def cyclic(value, axis, steps):
    count = lax.axis_size(axis)
    return lax.ppermute(value, axis, [(i, (i + steps) % count) for i in range(count)])


def swap(value, axis, bit):
    count = lax.axis_size(axis)
    return lax.ppermute(value, axis, [(i, i ^ bit) for i in range(count)])


def edge_rows(block):
    tiles = lax.axis_size("tile")
    if tiles == 2:
        mine = jnp.where(lax.axis_index("tile") == 0, block[:, -1:], block[:, :1])
        own = swap(mine, "tile", 1)
        blocks = lax.axis_size("tm")
        pairs = [(t * 2 + y, (t + 1) * 2 + 1 - y) for t in range(blocks - 1) for y in range(2)]
        before = lax.ppermute(mine, ("tm", "tile"), pairs)
        return own, own, before, before
    low = upward(block[:, -1:], "tile", 1)
    high = upward(block[:, :1], "tile", -1)
    return low, high, upward(low, "tm"), upward(high, "tm")


def share_stats(stats):
    if lax.axis_size("tile") == 2:
        both = jnp.stack([stats, swap(stats, "tile", 1)])
    else:
        both = lax.all_gather(stats, "tile", axis=0)
    return both, upward(both, "tm")


def whole_weights(shard):
    whole = lax.all_gather(shard, ("tm", "tile"), axis=2, tiled=True)
    return whole.reshape(-1, whole.shape[2]).T


def channel_stats(rows):
    mean = jnp.sum(rows, axis=0, keepdims=True) / rows.shape[0]
    centered = rows - mean
    return mean, jnp.sum(centered * centered, axis=0, keepdims=True)


def stats_kernel(x_ref, s_ref):
    frames, rows, columns, channels = x_ref.shape
    for f in range(frames):
        mean, spread = channel_stats(x_ref[f].astype(F32).reshape(rows * columns, channels))
        s_ref[f : f + 1] = mean
        s_ref[frames + f : frames + f + 1] = spread


def stats_of(block):
    frames, _, _, channels = block.shape
    return pl.pallas_call(
        stats_kernel,
        out_shape=jax.ShapeDtypeStruct((2 * frames, channels), F32),
        in_specs=[pl.BlockSpec(memory_space=pltpu.VMEM)],
        out_specs=pl.BlockSpec(memory_space=pltpu.VMEM),
        name="stats",
    )(block)


def norm_terms(stats, gain, cells):
    tiles, twice, channels = stats.shape
    frames = twice // 2
    width = channels // GROUPS
    a = lax.broadcasted_iota(jnp.int32, (channels, channels), 0) // width
    b = lax.broadcasted_iota(jnp.int32, (channels, channels), 1) // width
    same = jnp.where(a == b, 1.0, 0.0).astype(F32)
    pool = functools.partial(jnp.dot, precision=lax.Precision.HIGHEST, preferred_element_type=F32)
    mean = pool(jnp.sum(stats[:, :frames], axis=0), same) / (tiles * width)
    off = stats[:, :frames] - mean[None]
    spread = jnp.sum(stats[:, frames:] + cells * (off * off), axis=0)
    var = pool(spread, same) / (tiles * width * cells)
    return mean, lax.rsqrt(var + epsilon) * gain


def conv_kernel(n_weights, residual, *refs):
    own, prev, low_o, high_o, low_p, high_p, st_o, st_p, gain, bias = refs[:10]
    weights = refs[10 : 10 + n_weights]
    if residual:
        extra, out = refs[10 + n_weights : 12 + n_weights]
        wide, full, sems = refs[12 + n_weights :]
    else:
        out, stats_out = refs[10 + n_weights : 12 + n_weights]
        wide, full, sems = refs[12 + n_weights :]
    frames, rows, columns, channels = own.shape
    span = 3 * channels

    copies = [pltpu.make_async_copy(weights[0], full, sems.at[0])]
    for copy in copies:
        copy.start()

    cells = float(rows * columns)
    here = norm_terms(st_o[...], gain[...], cells)
    before = norm_terms(st_p[...], gain[...], cells)
    first_tile = lax.axis_index("tile") == 0
    last_tile = lax.axis_index("tile") == lax.axis_size("tile") - 1
    start = lax.axis_index("tm") == 0
    column = lax.broadcasted_iota(jnp.int32, (columns, channels), 0)

    def put(slot, row, raw, mean, scale, empty):
        half_y = (raw.astype(F32) - mean) * (0.5 * scale)
        y = half_y * (1.0 + jnp.tanh(half_y))
        if empty is not None:
            y = jnp.where(empty, 0.0, y)
        left = jnp.where(column == 0, 0.0, pltpu.roll(y, 1, 0))
        right = jnp.where(column == columns - 1, 0.0, pltpu.roll(y, columns - 1, 0))
        wide[slot, row, :, :channels] = left.astype(BF16)
        wide[slot, row, :, channels : 2 * channels] = y.astype(BF16)
        wide[slot, row, :, 2 * channels :] = right.astype(BF16)

    for f in range(2):
        mean, scale = here[0][f : f + 1], here[1][f : f + 1]

        def body(r, carry, f=f, mean=mean, scale=scale):
            put(2 + f, r + 1, own[f, r], mean, scale, None)
            return carry

        lax.fori_loop(0, rows, body, 0)
        put(2 + f, 0, low_o[f, 0], mean, scale, first_tile)
        put(2 + f, rows + 1, high_o[f, 0], mean, scale, last_tile)
    for f in range(2):
        mean, scale = before[0][f : f + 1], before[1][f : f + 1]

        def body(r, carry, f=f, mean=mean, scale=scale):
            put(f, r + 1, prev[f, r], mean, scale, start)
            return carry

        lax.fori_loop(0, rows, body, 0)
        put(f, 0, low_p[f, 0], mean, scale, start | first_tile)
        put(f, rows + 1, high_p[f, 0], mean, scale, start | last_tile)

    for copy in copies:
        copy.wait()

    def frame(f, carry):
        total = jnp.broadcast_to(bias[...], (rows * columns, channels))
        for df in range(3):
            for dh in range(3):
                left = wide[f + df, dh : dh + rows].reshape(rows * columns, span)
                at = (3 * df + dh) * span
                total = total + lax.dot_general(
                    left, full[:, at : at + span], NT, preferred_element_type=F32
                )
        if residual:
            total = total + extra[f].astype(F32).reshape(rows * columns, channels)
        done = total.astype(BF16)
        out[f] = done.reshape(rows, columns, channels)
        if not residual:
            mean, spread = channel_stats(done.astype(F32))
            stats_out[pl.ds(f, 1)] = mean
            stats_out[pl.ds(frames + f, 1)] = spread
        return carry

    lax.fori_loop(0, frames, frame, 0)


def conv(own, prev, edges, stats, gain, bias, weights, extra=None):
    frames, rows, columns, channels = own.shape
    vmem = pl.BlockSpec(memory_space=pltpu.VMEM)
    shapes = [jax.ShapeDtypeStruct(own.shape, BF16)]
    args = [own, prev, *edges, *stats, gain[None], bias[None], *weights]
    specs = [vmem] * 10 + [pl.BlockSpec(memory_space=pl.ANY)] * len(weights)
    if extra is None:
        shapes.append(jax.ShapeDtypeStruct((2 * frames, channels), F32))
    else:
        args.append(extra)
        specs.append(vmem)
    flops = 2 * frames * rows * columns * channels * channels * TAPS
    return pl.pallas_call(
        functools.partial(conv_kernel, len(weights), extra is not None),
        out_shape=shapes,
        in_specs=specs,
        out_specs=[vmem] * len(shapes),
        scratch_shapes=[
            pltpu.VMEM((4, rows + 2, columns, 3 * channels), BF16),
            pltpu.VMEM((channels, TAPS * channels), BF16),
            pltpu.SemaphoreType.DMA((1,)),
        ],
        cost_estimate=pl.CostEstimate(flops=flops, bytes_accessed=9 << 20, transcendentals=1 << 20),
        name="conv",
    )(*args)


def shards(latents, norm1_gain, conv1_weight, conv1_bias, norm2_gain, conv2_weight, conv2_bias):
    weights1 = [whole_weights(conv1_weight)]
    prev = upward(latents, "tm")
    edges = edge_rows(latents)
    stats = share_stats(stats_of(latents))
    hidden, sums = conv(latents, prev, edges, stats, norm1_gain, conv1_bias, weights1)
    weights2 = [whole_weights(conv2_weight)]
    prev = upward(hidden, "tm")
    edges = edge_rows(hidden)
    stats = share_stats(sums)
    return conv(hidden, prev, edges, stats, norm2_gain, conv2_bias, weights2, latents)[0]


HELD = (
    ((0, 0, 0), (1, 0, 0), (2, 0, 0), (3, 0, 0)),
    ((0, 0, 1), (1, 0, 1), (2, 0, 1), (3, 0, 1)),
    ((0, 1, 0), (1, 1, 0), (2, 1, 0), (3, 1, 0)),
    ((0, 1, 1), (1, 1, 1)),
    ((2, 1, 1), (3, 1, 1)),
)
NOTE = 16


def own_piece(shard):
    turned = jnp.swapaxes(shard, 1, 2)
    taps, outs, depth = turned.shape
    clip = lax.axis_index("clip")
    start = (0, (clip % 2) * (outs // 2), (clip // 2) * (depth // 2))
    return lax.dynamic_slice(turned, start, (taps, outs // 2, depth // 2))


def diagonal(note):
    blocks = lax.axis_size("tm")
    pairs = [(t * 2 + y, (t + 1) * 2 + 1 - y) for t in range(blocks - 1) for y in range(2)]
    return lax.ppermute(note, ("tm", "tile"), pairs)


def parts_of(value):
    first = value.astype(BF16).astype(F32)
    second = (value - first).astype(BF16).astype(F32)
    return [first, second, value - first - second]


def write_note(note, edge, mean, spread):
    columns, channels = edge.shape
    note[:columns] = edge
    lines = parts_of(mean) + parts_of(spread)
    lines.append(jnp.zeros((NOTE - 6, channels), F32))
    note[columns:] = jnp.concatenate(lines, axis=0).astype(BF16)


def read_note(note, columns):
    lines = note[columns:].astype(F32)
    mean = lines[0:1] + lines[1:2] + lines[2:3]
    spread = lines[3:4] + lines[4:5] + lines[5:6]
    return mean, spread


def notes_kernel(x_ref, note_ref):
    frames, rows, columns, channels = x_ref.shape
    at = jnp.where(lax.axis_index("tile") == 0, rows - 1, 0)
    for f in range(frames):
        mean, spread = channel_stats(x_ref[f].astype(F32).reshape(rows * columns, channels))
        write_note(note_ref.at[f], x_ref[f, at], mean, spread)


def notes_of(block):
    frames, _, columns, channels = block.shape
    return pl.pallas_call(
        notes_kernel,
        out_shape=jax.ShapeDtypeStruct((frames, columns + NOTE, channels), BF16),
        in_specs=[pl.BlockSpec(memory_space=pltpu.VMEM)],
        out_specs=pl.BlockSpec(memory_space=pltpu.VMEM),
        cost_estimate=pl.CostEstimate(flops=1 << 22, bytes_accessed=1 << 20, transcendentals=0),
        name="notes",
    )(block)


def part_kernel(plan, *refs):
    jobs, lo, hi = plan["jobs"], plan["lo"], plan["hi"]
    refs = dict(zip(plan["names"], refs))
    wide, full, sems = refs["wide"], refs["full"], refs["sems"]
    gain, bias = refs["gain"], refs["bias"]
    tm, tile, clip = (lax.axis_index(a) for a in ("tm", "tile", "clip"))
    rows, columns, channels = wide.shape[1] - 2, wide.shape[2], full.shape[1]
    cells = float(rows * columns)

    half, core = clip // 2, clip % 2
    copies = []
    for side in range(2):
        for group, names in enumerate(HELD):
            source = refs["w%d" % (side * len(HELD) + group)]
            high, deep = source.shape[2:]
            for at, (back, dy, dx) in enumerate(names):
                block = (lax.rem(tm + 4 - back, 4) * 2 + (tile ^ dy)) * 2 + (core ^ side)
                place = full.at[
                    :,
                    pl.ds(pl.multiple_of(block * high, high), high),
                    pl.ds(pl.multiple_of((half ^ dx) * deep, 128), deep),
                ]
                piece = source.at[at, pl.ds(lo, hi - lo)]
                copies.append(pltpu.make_async_copy(piece, place, sems.at[len(copies)]))
    for copy in copies:
        copy.start()

    slots = plan["slots"]
    means, spreads = [[], []], [[], []]
    for frame in slots:
        if frame >= 0:
            here = read_note(refs["note"].at[frame], columns)
            there = read_note(refs["other"].at[frame], columns)
        else:
            ref, at = plan["raw"][frame]
            raw = refs[ref][at].astype(F32).reshape(rows * columns, channels)
            here = channel_stats(raw)
            there = read_note(refs["before"].at[frame + 2], columns)
        for side, (mean, spread) in enumerate((here, there)):
            means[side].append(mean)
            spreads[side].append(spread)
    stats = jnp.stack([jnp.concatenate(means[s] + spreads[s], axis=0) for s in range(2)])
    mean_of, scale_of = norm_terms(stats, gain[...], cells)

    column = lax.broadcasted_iota(jnp.int32, (columns, channels), 0)

    def put(slot, row, raw, mean, scale, empty):
        half_y = (raw.astype(F32) - mean) * (0.5 * scale)
        y = half_y * (1.0 + jnp.tanh(half_y))
        if empty is not None:
            y = jnp.where(empty, 0.0, y)
        left = jnp.where(column == 0, 0.0, pltpu.roll(y, 1, 0))
        right = jnp.where(column == columns - 1, 0.0, pltpu.roll(y, columns - 1, 0))
        wide[slot, row, :, :channels] = left.astype(BF16)
        wide[slot, row, :, channels : 2 * channels] = y.astype(BF16)
        wide[slot, row, :, 2 * channels :] = right.astype(BF16)

    inner = jnp.where(tile == 0, rows + 1, 0)
    outer = jnp.where(tile == 0, 0, rows + 1)
    for slot, frame in enumerate(slots):
        mean, scale = mean_of[slot : slot + 1], scale_of[slot : slot + 1]
        ref, at = plan["raw"][frame]
        empty = None if frame >= 0 else tm == 0

        def body(r, carry, slot=slot, mean=mean, scale=scale, ref=ref, at=at, empty=empty):
            put(slot, r + 1, refs[ref][at, r], mean, scale, empty)
            return carry

        lax.fori_loop(0, rows, body, 0)
        edge = refs["other"][frame, :columns] if frame >= 0 else refs["before"][frame + 2, :columns]
        put(slot, inner, edge, mean, scale, empty)
        wide[slot, outer] = jnp.zeros((columns, 3 * channels), BF16)

    for copy in copies:
        copy.wait()

    for o, dfs in jobs.items():
        if "start" in refs:
            total = refs["start"][plan["start_at"][o]]
        else:
            total = jnp.broadcast_to(bias[...], (rows * columns, channels))
        for df in dfs:
            slot = slots.index(o + df - 2)
            for dh in range(3):
                left = wide[slot, dh : dh + rows].reshape(rows * columns, 3 * channels)
                tap = 9 * df + 3 * dh - lo
                right = jnp.concatenate([full[tap + i] for i in range(3)], axis=1)
                total = total + lax.dot_general(left, right, NT, preferred_element_type=F32)
        kind = plan["ends"][o]
        if kind == "partial":
            refs["partial"][plan["partial_at"][o]] = total
        elif kind == "hidden":
            done = total.astype(BF16)
            refs["out"][0] = done.reshape(rows, columns, channels)
            mean, spread = channel_stats(done.astype(F32))
            edge = refs["out"][0, jnp.where(tile == 0, rows - 1, 0)]
            write_note(refs["new"].at[plan["new_at"]], edge, mean, spread)
            if "keep" in refs:
                refs["new"][1] = refs["keep"][0]
        else:
            total = total + refs["extra"][o].astype(F32).reshape(rows * columns, channels)
            refs["out"][0] = total.astype(BF16).reshape(rows, columns, channels)


def part_conv(inputs, outputs, jobs, ends, raw, weights, aliases=None, **more):
    slots = sorted({o + df - 2 for o, dfs in jobs.items() for df in dfs})
    dfs = sorted({df for group in jobs.values() for df in group})
    lo, hi = 9 * dfs[0], 9 * (dfs[-1] + 1)
    inputs = {**inputs, **{"w%d" % i: w for i, w in enumerate(weights)}}
    _, rows, columns, channels = inputs[raw[slots[0]][0]].shape
    plan = dict(jobs=jobs, ends=ends, raw=raw, slots=slots, lo=lo, hi=hi, **more)
    plan["names"] = [*inputs, *outputs, "wide", "full", "sems"]
    vmem = pl.BlockSpec(memory_space=pltpu.VMEM)
    anywhere = pl.BlockSpec(memory_space=pl.ANY)
    aliases = aliases or {}
    out_specs = [vmem] * len(outputs)
    grid = ()
    if "out_at" in more:
        at, grid = more["out_at"], (1,)
        out_specs[0] = pl.BlockSpec((1, rows, columns, channels), lambda i: (at, 0, 0, 0))
    taps = sum(len(group) for group in jobs.values()) * 9
    return pl.pallas_call(
        functools.partial(part_kernel, plan),
        out_shape=list(outputs.values()),
        grid=grid,
        in_specs=[anywhere if name[0] == "w" or name in aliases else vmem for name in inputs],
        out_specs=out_specs,
        scratch_shapes=[
            pltpu.VMEM((len(slots), rows + 2, columns, 3 * channels), BF16),
            pltpu.VMEM((hi - lo, channels, channels), BF16),
            pltpu.SemaphoreType.DMA((32,)),
        ],
        input_output_aliases={
            list(inputs).index(source): list(outputs).index(target)
            for source, target in aliases.items()
        },
        cost_estimate=pl.CostEstimate(
            flops=2 * rows * columns * channels * channels * taps,
            bytes_accessed=6 << 20,
            transcendentals=rows * columns * channels * len(slots),
        ),
        name="conv_" + "_".join("%d%s" % (o, "".join(map(str, d))) for o, d in jobs.items()),
    )(*inputs.values())


def hold(*values):
    return lax.optimization_barrier(values)


def shards_fast(
    latents, norm1_gain, conv1_weight, conv1_bias, norm2_gain, conv2_weight, conv2_bias
):
    _, rows, columns, channels = latents.shape
    frame = jax.ShapeDtypeStruct((1, rows, columns, channels), BF16)
    block = jax.ShapeDtypeStruct(latents.shape, BF16)
    note = jax.ShapeDtypeStruct((1, columns + NOTE, channels), BF16)
    notes2 = jax.ShapeDtypeStruct((2, columns + NOTE, channels), BF16)
    sums = jax.ShapeDtypeStruct((2, rows * columns, channels), F32)
    sum1 = jax.ShapeDtypeStruct((1, rows * columns, channels), F32)
    gain1, bias1, gain2, bias2 = (
        v[None] for v in (norm1_gain, conv1_bias, norm2_gain, conv2_bias)
    )

    piece1, piece2 = own_piece(conv1_weight), own_piece(conv2_weight)
    turned1 = [cyclic(piece1, "tm", steps) for steps in (1, 2, 3)]
    notes = notes_of(latents)
    other = swap(notes, "tile", 1)
    before = diagonal(notes)
    turned1, other, before, latents_b = hold(turned1, other, before, latents)

    held1 = jnp.stack([piece1] + list(turned1))
    up1 = upward(latents_b[1:], "tm")
    across1 = swap(held1, "clip", 2)
    beside1 = swap(held1, "tile", 1)
    up1, across1, beside1, latents_c = hold(up1, across1, beside1, latents_b)

    up0 = upward(latents_c[:1], "tm")
    corner1a = swap(beside1[:2], "clip", 2)
    corner1b = swap(across1[2:], "tile", 1)
    weights1 = [held1, across1, beside1, corner1a, corner1b]
    weights1 = weights1 + [swap(a, "clip", 1) for a in weights1]
    first = dict(note=notes, other=other, before=before, gain=gain1, bias=bias1, own=latents)
    hidden1, note1 = part_conv(
        {**first, "odd": up1},
        {"out": frame, "new": note},
        {1: (0, 1, 2)},
        {1: "hidden"},
        {-1: ("odd", 0), 0: ("own", 0), 1: ("own", 1)},
        weights1,
        new_at=0,
    )

    up0, piece2_d = hold(up0, piece2)
    turned2 = [cyclic(piece2_d, "tm", steps) for steps in (1, 2, 3)]
    turned2, hidden1 = hold(turned2, hidden1)
    high1 = upward(hidden1, "tm")
    hidden0, notes_h = part_conv(
        {**first, "odd": up1, "even": up0, "keep": note1},
        {"out": frame, "new": notes2},
        {0: (0, 1, 2)},
        {0: "hidden"},
        {-2: ("even", 0), -1: ("odd", 0), 0: ("own", 0)},
        weights1,
        new_at=0,
    )
    held2 = jnp.stack([piece2] + list(turned2))
    across2 = swap(held2, "clip", 2)
    beside2 = swap(held2, "tile", 1)
    other_h = swap(notes_h, "tile", 1)
    before_h = diagonal(notes_h)
    across2, beside2, high1, hidden0 = hold(across2, beside2, high1, hidden0)

    high0 = upward(hidden0, "tm")
    corner2a = swap(beside2[:2], "clip", 2)
    corner2b = swap(across2[2:], "tile", 1)
    weights2 = [held2, across2, beside2, corner2a, corner2b]
    weights2 = weights2 + [swap(a, "clip", 1) for a in weights2]
    second = dict(note=notes_h, other=other_h, before=before_h, gain=gain2, bias=bias2)
    (partial,) = part_conv(
        {**second, "own0": hidden0, "own1": hidden1},
        {"partial": sums},
        {1: (1, 2), 0: (2,)},
        {1: "partial", 0: "partial"},
        {0: ("own0", 0), 1: ("own1", 0)},
        weights2,
        partial_at={0: 0, 1: 1},
    )
    out, partial = part_conv(
        {**second, "odd": high1, "own0": hidden0, "start": partial, "extra": latents},
        {"out": block, "partial": sum1},
        {1: (0,), 0: (1,)},
        {1: "final", 0: "partial"},
        {-1: ("odd", 0)},
        weights2,
        start_at={0: 0, 1: 1},
        partial_at={0: 0},
        out_at=1,
    )
    (out,) = part_conv(
        {**second, "even": high0, "start": partial, "extra": latents, "done": out},
        {"out": block},
        {0: (0,)},
        {0: "final"},
        {-2: ("even", 0)},
        weights2,
        aliases={"done": "out"},
        start_at={0: 0},
        out_at=0,
    )
    return out


def solution(mesh):
    placed = (
        P(("clip", "tm"), "tile", None, None),
        P(),
        P(None, None, ("tm", "tile")),
        P(),
        P(),
        P(None, None, ("tm", "tile")),
        P(),
    )
    sizes = tuple(mesh.shape[a] for a in ("tm", "tile", "clip"))
    return jax.shard_map(
        shards_fast if sizes == (4, 2, 4) else shards,
        mesh=mesh,
        in_specs=placed,
        out_specs=P(("clip", "tm"), "tile", None, None),
        check_vma=False,
    )
```

```python
import functools

import jax
import jax.numpy as jnp
from jax import lax
from jax.experimental import pallas as pl
from jax.experimental.pallas import tpu as pltpu
from jax.sharding import PartitionSpec as P

GROUPS = 32
TAPS = 27
epsilon = 1e-06
F32 = jnp.float32
BF16 = jnp.bfloat16
NT = (((1,), (1,)), ((), ()))


def upward(value, axis, steps=1):
    count = lax.axis_size(axis)
    first, last = (max(0, -steps), min(count, count - steps))
    return lax.ppermute(value, axis, [(source, source + steps) for source in range(first, last)])


def cyclic(value, axis, steps):
    count = lax.axis_size(axis)
    return lax.ppermute(value, axis, [(i, (i + steps) % count) for i in range(count)])


def swap(value, axis, bit):
    count = lax.axis_size(axis)
    return lax.ppermute(value, axis, [(i, i ^ bit) for i in range(count)])


def edge_rows(block):
    tiles = lax.axis_size("tile")
    if tiles == 2:
        mine = jnp.where(lax.axis_index("tile") == 0, block[:, -1:], block[:, :1])
        own = swap(mine, "tile", 1)
        blocks = lax.axis_size("tm")
        pairs = [(t * 2 + y, (t + 1) * 2 + 1 - y) for t in range(blocks - 1) for y in range(2)]
        before = lax.ppermute(mine, ("tm", "tile"), pairs)
        return own, own, before, before
    low = upward(block[:, -1:], "tile", 1)
    high = upward(block[:, :1], "tile", -1)
    return low, high, upward(low, "tm"), upward(high, "tm")


def share_stats(stats):
    if lax.axis_size("tile") == 2:
        both = jnp.stack([stats, swap(stats, "tile", 1)])
    else:
        both = lax.all_gather(stats, "tile", axis=0)
    return both, upward(both, "tm")


def whole_weights(shard):
    whole = lax.all_gather(shard, ("tm", "tile"), axis=2, tiled=True)
    return whole.reshape(-1, whole.shape[2]).T


def channel_stats(rows):
    mean = jnp.sum(rows, axis=0, keepdims=True) / rows.shape[0]
    centered = rows - mean
    return mean, jnp.sum(centered * centered, axis=0, keepdims=True)


def stats_kernel(x_ref, s_ref):
    frames, rows, columns, channels = x_ref.shape
    for f in range(frames):
        mean, spread = channel_stats(x_ref[f].astype(F32).reshape(rows * columns, channels))
        s_ref[f : f + 1] = mean
        s_ref[frames + f : frames + f + 1] = spread


def stats_of(block):
    frames, _, _, channels = block.shape
    return pl.pallas_call(
        stats_kernel,
        out_shape=jax.ShapeDtypeStruct((2 * frames, channels), F32),
        in_specs=[pl.BlockSpec(memory_space=pltpu.VMEM)],
        out_specs=pl.BlockSpec(memory_space=pltpu.VMEM),
        name="stats",
    )(block)


def norm_terms(stats, gain, cells):
    tiles, twice, channels = stats.shape
    frames = twice // 2
    width = channels // GROUPS
    a = lax.broadcasted_iota(jnp.int32, (channels, channels), 0) // width
    b = lax.broadcasted_iota(jnp.int32, (channels, channels), 1) // width
    same = jnp.where(a == b, 1.0, 0.0).astype(F32)
    pool = functools.partial(jnp.dot, precision=lax.Precision.HIGHEST, preferred_element_type=F32)
    mean = pool(jnp.sum(stats[:, :frames], axis=0), same) / (tiles * width)
    off = stats[:, :frames] - mean[None]
    spread = jnp.sum(stats[:, frames:] + cells * (off * off), axis=0)
    var = pool(spread, same) / (tiles * width * cells)
    return mean, lax.rsqrt(var + epsilon) * gain


def pool_terms(stats, gain, cells):
    tiles, twice, channels = stats.shape
    frames = twice // 2
    width = channels // GROUPS
    a = lax.broadcasted_iota(jnp.int32, (channels, channels), 0) // width
    b = lax.broadcasted_iota(jnp.int32, (channels, channels), 1) // width
    same = jnp.where(a == b, 1.0, 0.0).astype(BF16)

    def pool(value):
        parts = jnp.concatenate(parts_of(value), axis=0).astype(BF16)
        sums = jnp.dot(parts, same, preferred_element_type=F32)
        return sums[:frames] + sums[frames : 2 * frames] + sums[2 * frames :]

    mean = pool(jnp.sum(stats[:, :frames], axis=0)) / (tiles * width)
    off = stats[:, :frames] - mean[None]
    spread = jnp.sum(stats[:, frames:] + cells * (off * off), axis=0)
    var = pool(spread) / (tiles * width * cells)
    return mean, lax.rsqrt(var + epsilon) * gain


def conv_kernel(n_weights, residual, *refs):
    own, prev, low_o, high_o, low_p, high_p, st_o, st_p, gain, bias = refs[:10]
    weights = refs[10 : 10 + n_weights]
    if residual:
        extra, out = refs[10 + n_weights : 12 + n_weights]
        wide, full, sems = refs[12 + n_weights :]
    else:
        out, stats_out = refs[10 + n_weights : 12 + n_weights]
        wide, full, sems = refs[12 + n_weights :]
    frames, rows, columns, channels = own.shape
    span = 3 * channels

    copies = [pltpu.make_async_copy(weights[0], full, sems.at[0])]
    for copy in copies:
        copy.start()

    cells = float(rows * columns)
    here = norm_terms(st_o[...], gain[...], cells)
    before = norm_terms(st_p[...], gain[...], cells)
    first_tile = lax.axis_index("tile") == 0
    last_tile = lax.axis_index("tile") == lax.axis_size("tile") - 1
    start = lax.axis_index("tm") == 0
    column = lax.broadcasted_iota(jnp.int32, (columns, channels), 0)

    def put(slot, row, raw, mean, scale, empty):
        half_y = (raw.astype(F32) - mean) * (0.5 * scale)
        y = half_y * (1.0 + jnp.tanh(half_y))
        if empty is not None:
            y = jnp.where(empty, 0.0, y)
        left = jnp.where(column == 0, 0.0, pltpu.roll(y, 1, 0))
        right = jnp.where(column == columns - 1, 0.0, pltpu.roll(y, columns - 1, 0))
        wide[slot, row, :, :channels] = left.astype(BF16)
        wide[slot, row, :, channels : 2 * channels] = y.astype(BF16)
        wide[slot, row, :, 2 * channels :] = right.astype(BF16)

    for f in range(2):
        mean, scale = here[0][f : f + 1], here[1][f : f + 1]

        def body(r, carry, f=f, mean=mean, scale=scale):
            put(2 + f, r + 1, own[f, r], mean, scale, None)
            return carry

        lax.fori_loop(0, rows, body, 0)
        put(2 + f, 0, low_o[f, 0], mean, scale, first_tile)
        put(2 + f, rows + 1, high_o[f, 0], mean, scale, last_tile)
    for f in range(2):
        mean, scale = before[0][f : f + 1], before[1][f : f + 1]

        def body(r, carry, f=f, mean=mean, scale=scale):
            put(f, r + 1, prev[f, r], mean, scale, start)
            return carry

        lax.fori_loop(0, rows, body, 0)
        put(f, 0, low_p[f, 0], mean, scale, start | first_tile)
        put(f, rows + 1, high_p[f, 0], mean, scale, start | last_tile)

    for copy in copies:
        copy.wait()

    def frame(f, carry):
        total = jnp.broadcast_to(bias[...], (rows * columns, channels))
        for df in range(3):
            for dh in range(3):
                left = wide[f + df, dh : dh + rows].reshape(rows * columns, span)
                at = (3 * df + dh) * span
                total = total + lax.dot_general(
                    left, full[:, at : at + span], NT, preferred_element_type=F32
                )
        if residual:
            total = total + extra[f].astype(F32).reshape(rows * columns, channels)
        done = total.astype(BF16)
        out[f] = done.reshape(rows, columns, channels)
        if not residual:
            mean, spread = channel_stats(done.astype(F32))
            stats_out[pl.ds(f, 1)] = mean
            stats_out[pl.ds(frames + f, 1)] = spread
        return carry

    lax.fori_loop(0, frames, frame, 0)


def conv(own, prev, edges, stats, gain, bias, weights, extra=None):
    frames, rows, columns, channels = own.shape
    vmem = pl.BlockSpec(memory_space=pltpu.VMEM)
    shapes = [jax.ShapeDtypeStruct(own.shape, BF16)]
    args = [own, prev, *edges, *stats, gain[None], bias[None], *weights]
    specs = [vmem] * 10 + [pl.BlockSpec(memory_space=pl.ANY)] * len(weights)
    if extra is None:
        shapes.append(jax.ShapeDtypeStruct((2 * frames, channels), F32))
    else:
        args.append(extra)
        specs.append(vmem)
    flops = 2 * frames * rows * columns * channels * channels * TAPS
    return pl.pallas_call(
        functools.partial(conv_kernel, len(weights), extra is not None),
        out_shape=shapes,
        in_specs=specs,
        out_specs=[vmem] * len(shapes),
        scratch_shapes=[
            pltpu.VMEM((4, rows + 2, columns, 3 * channels), BF16),
            pltpu.VMEM((channels, TAPS * channels), BF16),
            pltpu.SemaphoreType.DMA((1,)),
        ],
        cost_estimate=pl.CostEstimate(flops=flops, bytes_accessed=9 << 20, transcendentals=1 << 20),
        name="conv",
    )(*args)


def shards(latents, norm1_gain, conv1_weight, conv1_bias, norm2_gain, conv2_weight, conv2_bias):
    weights1 = [whole_weights(conv1_weight)]
    prev = upward(latents, "tm")
    edges = edge_rows(latents)
    stats = share_stats(stats_of(latents))
    hidden, sums = conv(latents, prev, edges, stats, norm1_gain, conv1_bias, weights1)
    weights2 = [whole_weights(conv2_weight)]
    prev = upward(hidden, "tm")
    edges = edge_rows(hidden)
    stats = share_stats(sums)
    return conv(hidden, prev, edges, stats, norm2_gain, conv2_bias, weights2, latents)[0]


HELD = {
    8: (
        ((0, 0, 0),),
        ((1, 0, 0), (2, 0, 0), (3, 0, 0)),
        ((0, 0, 1),),
        ((0, 1, 0),),
        ((1, 0, 1), (2, 0, 1), (3, 0, 1)),
        ((1, 1, 0), (2, 1, 0), (3, 1, 0)),
        ((0, 1, 1), (1, 1, 1)),
        ((2, 1, 1), (3, 1, 1)),
    ),
    5: (
        ((0, 0, 0), (1, 0, 0), (2, 0, 0), (3, 0, 0)),
        ((0, 0, 1), (1, 0, 1), (2, 0, 1), (3, 0, 1)),
        ((0, 1, 0), (1, 1, 0), (2, 1, 0), (3, 1, 0)),
        ((0, 1, 1), (1, 1, 1)),
        ((2, 1, 1), (3, 1, 1)),
    ),
}
BLOCK = 512
NOTE = 16


def own_piece(shard):
    turned = jnp.swapaxes(shard, 1, 2)
    taps, outs, depth = turned.shape
    clip = lax.axis_index("clip")
    start = (0, (clip % 2) * (outs // 2), (clip // 2) * (depth // 2))
    return lax.dynamic_slice(turned, start, (taps, outs // 2, depth // 2))


def diagonal(note):
    blocks = lax.axis_size("tm")
    pairs = [(t * 2 + y, (t + 1) * 2 + 1 - y) for t in range(blocks - 1) for y in range(2)]
    return lax.ppermute(note, ("tm", "tile"), pairs)


def parts_of(value):
    first = value.astype(BF16).astype(F32)
    second = (value - first).astype(BF16).astype(F32)
    return [first, second, value - first - second]


def write_note(note, edge, mean, spread):
    columns, channels = edge.shape
    note[:columns] = edge
    lines = parts_of(mean) + parts_of(spread)
    lines.append(jnp.zeros((NOTE - 6, channels), F32))
    note[columns:] = jnp.concatenate(lines, axis=0).astype(BF16)


def read_note(lines):
    lines = lines.astype(F32)
    mean = lines[0:1] + lines[1:2] + lines[2:3]
    spread = lines[3:4] + lines[4:5] + lines[5:6]
    return mean, spread


def frame_stats(frame):
    rows, columns, channels = frame.shape

    def total(of):
        def body(r, carry):
            value = of(frame[r].astype(F32))
            return carry + jnp.sum(value.reshape(columns // 8, 8, channels), axis=0)

        lines = lax.fori_loop(0, rows, body, jnp.zeros((8, channels), F32))
        return jnp.sum(lines, axis=0, keepdims=True)

    mean = total(lambda x: x) / (rows * columns)

    def squared(x):
        centered = x - mean
        return centered * centered

    return mean, total(squared)


def notes_kernel(x_ref, note_ref):
    frames, rows, columns, channels = x_ref.shape
    at = jnp.where(lax.axis_index("tile") == 0, rows - 1, 0)
    for f in range(frames):
        mean, spread = frame_stats(x_ref.at[f])
        write_note(note_ref.at[f], x_ref[f, at], mean, spread)


def notes_of(block):
    frames, _, columns, channels = block.shape
    return pl.pallas_call(
        notes_kernel,
        out_shape=jax.ShapeDtypeStruct((frames, columns + NOTE, channels), BF16),
        in_specs=[pl.BlockSpec(memory_space=pltpu.VMEM)],
        out_specs=pl.BlockSpec(memory_space=pltpu.VMEM),
        cost_estimate=pl.CostEstimate(flops=1 << 34, bytes_accessed=1 << 10, transcendentals=0),
        name="notes",
    )(block)


def part_kernel(plan, *refs):
    jobs, lo, hi = plan["jobs"], plan["lo"], plan["hi"]
    refs = dict(zip(plan["names"], refs))
    wide, full, sems = refs["wide"], refs["full"], refs["sems"]
    tm, tile, clip = (lax.axis_index(a) for a in ("tm", "tile", "clip"))
    rows, columns, channels = wide.shape[1] - 2, wide.shape[2], full.shape[1]
    cells = float(rows * columns)

    half, core = clip // 2, clip % 2
    copies = []
    for side in range(2):
        for group, names in enumerate(HELD[plan["groups"]]):
            source = refs["w%d" % (side * plan["groups"] + group)]
            high, deep = source.shape[2:]
            for at, (back, dy, dx) in enumerate(names):
                block = (lax.rem(tm + 4 - back, 4) * 2 + (tile ^ dy)) * 2 + (core ^ side)
                place = full.at[
                    :,
                    pl.ds(pl.multiple_of(block * high, high), high),
                    pl.ds(pl.multiple_of((half ^ dx) * deep, 128), deep),
                ]
                piece = source.at[at, pl.ds(lo, hi - lo)]
                copies.append(pltpu.make_async_copy(piece, place, sems.at[len(copies)]))
    slots = plan["slots"]
    count = len(copies)
    early, late = [], []

    def fetch(group, source, place):
        group.append(pltpu.make_async_copy(source, place, sems.at[count + len(early) + len(late)]))
        group[-1].start()

    inner = jnp.where(tile == 0, rows + 1, 0)
    outer = jnp.where(tile == 0, 0, rows + 1)
    fetch(early, refs["vector"], refs["pair"])
    for slot, frame in enumerate(slots):
        ref, at = plan["raw"][frame]
        if len(refs[ref].shape) == 2:
            for r in range(rows):
                line = refs[ref].at[pl.ds(r * columns, columns)]
                fetch(early, line, refs["raw"].at[slot, r + 1])
            near = refs[ref].at[pl.ds(rows * columns, columns + NOTE)]
        else:
            fetch(early, refs[ref].at[at], refs["raw"].at[slot, pl.ds(1, rows)])
            near = refs["other"].at[frame] if frame >= 0 else refs["before"].at[frame + 2]
        fetch(early, near.at[pl.ds(0, columns)], refs["raw"].at[slot, inner])
        fetch(early, near.at[pl.ds(columns, NOTE)], refs["lines"].at[1, slot])
        if frame >= 0:
            lines = refs["note"].at[frame, pl.ds(columns, NOTE)]
            fetch(early, lines, refs["lines"].at[0, slot])
    for copy in copies:
        copy.start()
    for o in jobs:
        if "start" in refs:
            fetch(late, refs["start"].at[o], refs["sum"].at[o])
        if plan["ends"][o] == "final":
            fetch(late, refs["extra"].at[o], refs["rest"].at[o])
    for copy in early:
        copy.wait()

    means, spreads = [[], []], [[], []]
    for slot, frame in enumerate(slots):
        if frame >= 0:
            here = read_note(refs["lines"][0, slot])
        else:
            here = frame_stats(refs["raw"].at[slot, pl.ds(1, rows)])
        there = read_note(refs["lines"][1, slot])
        for side, (mean, spread) in enumerate((here, there)):
            means[side].append(mean)
            spreads[side].append(spread)
    stats = jnp.stack([jnp.concatenate(means[s] + spreads[s], axis=0) for s in range(2)])
    mean_of, scale_of = pool_terms(stats, refs["pair"][0:1], cells)
    for slot in range(len(slots)):
        refs["terms"][slot, 0:1] = mean_of[slot : slot + 1]
        refs["terms"][slot, 1:2] = scale_of[slot : slot + 1] * 0.5
        wide[slot, outer] = jnp.zeros((columns, 3 * channels), BF16)

    column = lax.broadcasted_iota(jnp.int32, (columns, channels), 0)
    halos = sum(frame < 0 for frame in slots)
    shown = rows + 1

    def put(i, carry):
        slot = i // shown
        row = i % shown + jnp.where(tile == 0, 1, 0)
        x = refs["raw"][slot, row].astype(F32)
        half_y = (x - refs["terms"][slot, 0:1]) * refs["terms"][slot, 1:2]
        y = half_y * (1.0 + jnp.tanh(half_y))
        if halos:
            y = jnp.where((slot < halos) & (tm == 0), 0.0, y)
        left = jnp.where(column == 0, 0.0, pltpu.roll(y, 1, 0))
        right = jnp.where(column == columns - 1, 0.0, pltpu.roll(y, columns - 1, 0))
        wide[slot, row, :, :channels] = left.astype(BF16)
        wide[slot, row, :, channels : 2 * channels] = y.astype(BF16)
        wide[slot, row, :, 2 * channels :] = right.astype(BF16)
        return carry

    lax.fori_loop(0, len(slots) * shown, put, 0, unroll=1)

    for copy in copies + late:
        copy.wait()

    step = BLOCK // columns
    leaving = []
    for o, dfs in jobs.items():
        kind = plan["ends"][o]

        def leave(m, o=o):
            here = pl.ds(m * step, step)
            spot = refs["done_at"].at[o, here]
            place = refs["out"].at[o, here]
            return pltpu.make_async_copy(spot, place, refs["done_sem"].at[o * rows + m])

        def block(m, carry, o=o, dfs=dfs, kind=kind, leave=leave):
            here = pl.ds(m * step, step)
            flat = pl.ds(pl.multiple_of(m * BLOCK, BLOCK), BLOCK)
            if "start" in refs:
                total = refs["sum"][o, flat]
            else:
                total = jnp.broadcast_to(refs["pair"][1:2], (BLOCK, channels))
            for df in dfs:
                slot = slots.index(o + df - 2)
                for dh in range(3):
                    left = wide[slot, pl.ds(dh + m * step, step)].reshape(BLOCK, 3 * channels)
                    tap = 9 * df + 3 * dh - lo
                    right = jnp.concatenate([full[tap + i] for i in range(3)], axis=1)
                    total = total + lax.dot_general(left, right, NT, preferred_element_type=F32)
            if kind == "partial":
                refs["partial"][o, flat] = total
                return carry
            if kind == "final":
                total = total + refs["rest"][o, here].astype(F32).reshape(BLOCK, channels)
            refs["done_at"][o, here] = total.astype(BF16).reshape(step, columns, channels)
            leave(m).start()
            return carry

        lax.fori_loop(0, rows // step, block, 0)
        if kind == "hidden":
            mean, spread = frame_stats(refs["done_at"].at[o])
            edge = refs["done_at"][o, jnp.where(tile == 0, rows - 1, 0)]
            write_note(refs["new"].at[o], edge, mean, spread)
        if kind != "partial":
            leaving += [leave(m) for m in range(rows // step)]
    for copy in leaving:
        copy.wait()


def part_conv(inputs, outputs, jobs, ends, raw, weights, aliases=None, cost=1 << 10, **more):
    slots = sorted({o + df - 2 for o, dfs in jobs.items() for df in dfs})
    dfs = sorted({df for group in jobs.values() for df in group})
    lo, hi = 9 * dfs[0], 9 * (dfs[-1] + 1)
    inputs = {**inputs, **{"w%d" % i: w for i, w in enumerate(weights)}}
    _, rows, columns, channels = inputs[next(n for n in ("own", "extra") if n in inputs)].shape
    plan = dict(groups=len(weights) // 2, jobs=jobs, ends=ends, raw=raw, slots=slots, lo=lo, hi=hi, **more)
    scratch = ["wide", "full", "sems", "raw", "lines", "sum", "rest", "terms", "pair", "done_at", "done_sem"]
    plan["names"] = [*inputs, *outputs, *scratch]
    small = ()
    vmem = pl.BlockSpec(memory_space=pltpu.VMEM)
    anywhere = pl.BlockSpec(memory_space=pl.ANY)
    aliases = aliases or {}
    out_specs = [anywhere if name == "out" else vmem for name in outputs]
    return pl.pallas_call(
        functools.partial(part_kernel, plan),
        out_shape=list(outputs.values()),
        in_specs=[vmem if name in small else anywhere for name in inputs],
        out_specs=out_specs,
        scratch_shapes=[
            pltpu.VMEM((len(slots), rows + 2, columns, 3 * channels), BF16),
            pltpu.VMEM((hi - lo, channels, channels), BF16),
            pltpu.SemaphoreType.DMA((80,)),
            pltpu.VMEM((len(slots), rows + 2, columns, channels), BF16),
            pltpu.VMEM((2, len(slots), NOTE, channels), BF16),
            pltpu.VMEM((len(jobs) if "start" in inputs else 1, rows * columns, channels), F32),
            pltpu.VMEM((len(jobs), rows, columns, channels), BF16),
            pltpu.VMEM((len(slots), 8, channels), F32),
            pltpu.VMEM((2, channels), F32),
            pltpu.VMEM((len(jobs), rows, columns, channels), F32 if "out" not in outputs else BF16),
            pltpu.SemaphoreType.DMA((2 * rows,)),
        ],
        input_output_aliases={
            list(inputs).index(source): list(outputs).index(target)
            for source, target in aliases.items()
        },
        cost_estimate=pl.CostEstimate(
            flops=cost,
            bytes_accessed=1 << 10,
            transcendentals=0,
        ),
        name="conv_" + "_".join("%d%s" % (o, "".join(map(str, d))) for o, d in jobs.items()),
    )(*inputs.values())


def along_tm(quarter):
    return [cyclic(quarter, "tm", steps) for steps in (3, 2, 1)][::-1]


def both_cores(arrays):
    return arrays + [swap(a, "clip", 1) for a in arrays]


def hold(*values):
    return lax.optimization_barrier(values)


def shards_fast(
    latents, norm1_gain, conv1_weight, conv1_bias, norm2_gain, conv2_weight, conv2_bias
):
    _, rows, columns, channels = latents.shape
    block = jax.ShapeDtypeStruct(latents.shape, BF16)
    notes_like = jax.ShapeDtypeStruct((2, columns + NOTE, channels), BF16)
    sums = jax.ShapeDtypeStruct((2, rows * columns, channels), F32)
    vector1 = jnp.stack([norm1_gain, conv1_bias])
    vector2 = jnp.stack([norm2_gain, conv2_bias])

    quarter1, quarter2 = own_piece(conv1_weight)[None], own_piece(conv2_weight)[None]
    turned = along_tm(quarter1)
    near1 = swap(quarter1, "clip", 2), swap(quarter1, "tile", 1)
    quarter1_n, latents_n = hold(quarter1, latents)
    notes = notes_of(latents_n)
    other = swap(notes, "tile", 1)
    turned, near1, other, latents_b = hold(turned, near1, other, latents)

    flat = latents_b.reshape(2, rows * columns, channels)
    send1 = jnp.concatenate([flat[1], other[1]])
    send0 = jnp.concatenate([flat[0], other[0]])
    up1 = upward(send1, "tm")
    up0 = upward(send0, "tm")
    held1 = jnp.concatenate(turned)
    far1 = swap(held1, "clip", 2), swap(held1, "tile", 1)
    far1, up1 = hold(far1, up1)

    corners1 = (
        swap(jnp.concatenate([near1[1], far1[1][:1]]), "clip", 2),
        swap(far1[0][1:], "tile", 1),
    )
    weights1 = both_cores([quarter1, held1, *near1, *far1, *corners1])
    weights1, up0, quarter2 = hold(weights1, up0, quarter2)
    turned2 = along_tm(quarter2)
    hidden, notes_h = part_conv(
        dict(note=notes, other=other, vector=vector1, own=latents, odd=up1, even=up0),
        {"out": block, "new": notes_like},
        {1: (0, 1, 2), 0: (0, 1, 2)},
        {1: "hidden", 0: "hidden"},
        {-2: ("even", 0), -1: ("odd", 0), 0: ("own", 0), 1: ("own", 1)},
        weights1,
        cost=1 << 34,
    )

    other_h = swap(notes_h, "tile", 1)
    before_h = diagonal(notes_h)
    before_h, hidden_d = hold(before_h, hidden)
    high = upward(hidden_d, "tm")
    held2 = jnp.concatenate([quarter2, *turned2])
    far2 = swap(held2, "clip", 2), swap(held2, "tile", 1)
    corners2 = swap(far2[1][:2], "clip", 2), swap(far2[0][2:], "tile", 1)
    weights2 = both_cores([held2, *far2, *corners2])
    (out,) = part_conv(
        dict(
            note=notes_h, other=other_h, before=before_h, vector=vector2, own=hidden,
            halo=high, extra=latents,
        ),
        {"out": block},
        {1: (0, 1, 2), 0: (0, 1, 2)},
        {1: "final", 0: "final"},
        {-2: ("halo", 0), -1: ("halo", 1), 0: ("own", 0), 1: ("own", 1)},
        weights2,
    )
    return out


def solution(mesh):
    placed = (
        P(("clip", "tm"), "tile", None, None),
        P(),
        P(None, None, ("tm", "tile")),
        P(),
        P(),
        P(None, None, ("tm", "tile")),
        P(),
    )
    sizes = tuple(mesh.shape[a] for a in ("tm", "tile", "clip"))
    return jax.shard_map(
        shards_fast if sizes == (4, 2, 4) else shards,
        mesh=mesh,
        in_specs=placed,
        out_specs=P(("clip", "tm"), "tile", None, None),
        check_vma=False,
    )
```

```python
import functools

import jax
import jax.numpy as jnp
from jax import lax
from jax.experimental import pallas as pl
from jax.experimental.pallas import tpu as pltpu
from jax.sharding import PartitionSpec as P

GROUPS = 32
TAPS = 27
epsilon = 1e-06
F32 = jnp.float32
BF16 = jnp.bfloat16
NT = (((1,), (1,)), ((), ()))


def upward(value, axis, steps=1):
    count = lax.axis_size(axis)
    first, last = (max(0, -steps), min(count, count - steps))
    return lax.ppermute(value, axis, [(source, source + steps) for source in range(first, last)])


def cyclic(value, axis, steps):
    count = lax.axis_size(axis)
    return lax.ppermute(value, axis, [(i, (i + steps) % count) for i in range(count)])


def swap(value, axis, bit):
    count = lax.axis_size(axis)
    return lax.ppermute(value, axis, [(i, i ^ bit) for i in range(count)])


def edge_rows(block):
    tiles = lax.axis_size("tile")
    if tiles == 2:
        mine = jnp.where(lax.axis_index("tile") == 0, block[:, -1:], block[:, :1])
        own = swap(mine, "tile", 1)
        blocks = lax.axis_size("tm")
        pairs = [(t * 2 + y, (t + 1) * 2 + 1 - y) for t in range(blocks - 1) for y in range(2)]
        before = lax.ppermute(mine, ("tm", "tile"), pairs)
        return own, own, before, before
    low = upward(block[:, -1:], "tile", 1)
    high = upward(block[:, :1], "tile", -1)
    return low, high, upward(low, "tm"), upward(high, "tm")


def share_stats(stats):
    if lax.axis_size("tile") == 2:
        both = jnp.stack([stats, swap(stats, "tile", 1)])
    else:
        both = lax.all_gather(stats, "tile", axis=0)
    return both, upward(both, "tm")


def whole_weights(shard):
    whole = lax.all_gather(shard, ("tm", "tile"), axis=2, tiled=True)
    return whole.reshape(-1, whole.shape[2]).T


def channel_stats(rows):
    mean = jnp.sum(rows, axis=0, keepdims=True) / rows.shape[0]
    centered = rows - mean
    return mean, jnp.sum(centered * centered, axis=0, keepdims=True)


def stats_kernel(x_ref, s_ref):
    frames, rows, columns, channels = x_ref.shape
    for f in range(frames):
        mean, spread = channel_stats(x_ref[f].astype(F32).reshape(rows * columns, channels))
        s_ref[f : f + 1] = mean
        s_ref[frames + f : frames + f + 1] = spread


def stats_of(block):
    frames, _, _, channels = block.shape
    return pl.pallas_call(
        stats_kernel,
        out_shape=jax.ShapeDtypeStruct((2 * frames, channels), F32),
        in_specs=[pl.BlockSpec(memory_space=pltpu.VMEM)],
        out_specs=pl.BlockSpec(memory_space=pltpu.VMEM),
        name="stats",
    )(block)


def norm_terms(stats, gain, cells):
    tiles, twice, channels = stats.shape
    frames = twice // 2
    width = channels // GROUPS
    a = lax.broadcasted_iota(jnp.int32, (channels, channels), 0) // width
    b = lax.broadcasted_iota(jnp.int32, (channels, channels), 1) // width
    same = jnp.where(a == b, 1.0, 0.0).astype(F32)
    pool = functools.partial(jnp.dot, precision=lax.Precision.HIGHEST, preferred_element_type=F32)
    mean = pool(jnp.sum(stats[:, :frames], axis=0), same) / (tiles * width)
    off = stats[:, :frames] - mean[None]
    spread = jnp.sum(stats[:, frames:] + cells * (off * off), axis=0)
    var = pool(spread, same) / (tiles * width * cells)
    return mean, lax.rsqrt(var + epsilon) * gain


def pool_terms(stats, gain, cells):
    tiles, twice, channels = stats.shape
    frames = twice // 2
    width = channels // GROUPS
    a = lax.broadcasted_iota(jnp.int32, (channels, channels), 0) // width
    b = lax.broadcasted_iota(jnp.int32, (channels, channels), 1) // width
    same = jnp.where(a == b, 1.0, 0.0).astype(BF16)

    def pool(value):
        parts = jnp.concatenate(parts_of(value), axis=0).astype(BF16)
        sums = jnp.dot(parts, same, preferred_element_type=F32)
        return sums[:frames] + sums[frames : 2 * frames] + sums[2 * frames :]

    mean = pool(jnp.sum(stats[:, :frames], axis=0)) / (tiles * width)
    off = stats[:, :frames] - mean[None]
    spread = jnp.sum(stats[:, frames:] + cells * (off * off), axis=0)
    var = pool(spread) / (tiles * width * cells)
    return mean, lax.rsqrt(var + epsilon) * gain


def conv_kernel(n_weights, residual, *refs):
    own, prev, low_o, high_o, low_p, high_p, st_o, st_p, gain, bias = refs[:10]
    weights = refs[10 : 10 + n_weights]
    if residual:
        extra, out = refs[10 + n_weights : 12 + n_weights]
        wide, full, sems = refs[12 + n_weights :]
    else:
        out, stats_out = refs[10 + n_weights : 12 + n_weights]
        wide, full, sems = refs[12 + n_weights :]
    frames, rows, columns, channels = own.shape
    span = 3 * channels

    copies = [pltpu.make_async_copy(weights[0], full, sems.at[0])]
    for copy in copies:
        copy.start()

    cells = float(rows * columns)
    here = norm_terms(st_o[...], gain[...], cells)
    before = norm_terms(st_p[...], gain[...], cells)
    first_tile = lax.axis_index("tile") == 0
    last_tile = lax.axis_index("tile") == lax.axis_size("tile") - 1
    start = lax.axis_index("tm") == 0
    column = lax.broadcasted_iota(jnp.int32, (columns, channels), 0)

    def put(slot, row, raw, mean, scale, empty):
        half_y = (raw.astype(F32) - mean) * (0.5 * scale)
        y = half_y * (1.0 + jnp.tanh(half_y))
        if empty is not None:
            y = jnp.where(empty, 0.0, y)
        left = jnp.where(column == 0, 0.0, pltpu.roll(y, 1, 0))
        right = jnp.where(column == columns - 1, 0.0, pltpu.roll(y, columns - 1, 0))
        wide[slot, row, :, :channels] = left.astype(BF16)
        wide[slot, row, :, channels : 2 * channels] = y.astype(BF16)
        wide[slot, row, :, 2 * channels :] = right.astype(BF16)

    for f in range(2):
        mean, scale = here[0][f : f + 1], here[1][f : f + 1]

        def body(r, carry, f=f, mean=mean, scale=scale):
            put(2 + f, r + 1, own[f, r], mean, scale, None)
            return carry

        lax.fori_loop(0, rows, body, 0)
        put(2 + f, 0, low_o[f, 0], mean, scale, first_tile)
        put(2 + f, rows + 1, high_o[f, 0], mean, scale, last_tile)
    for f in range(2):
        mean, scale = before[0][f : f + 1], before[1][f : f + 1]

        def body(r, carry, f=f, mean=mean, scale=scale):
            put(f, r + 1, prev[f, r], mean, scale, start)
            return carry

        lax.fori_loop(0, rows, body, 0)
        put(f, 0, low_p[f, 0], mean, scale, start | first_tile)
        put(f, rows + 1, high_p[f, 0], mean, scale, start | last_tile)

    for copy in copies:
        copy.wait()

    def frame(f, carry):
        total = jnp.broadcast_to(bias[...], (rows * columns, channels))
        for df in range(3):
            for dh in range(3):
                left = wide[f + df, dh : dh + rows].reshape(rows * columns, span)
                at = (3 * df + dh) * span
                total = total + lax.dot_general(
                    left, full[:, at : at + span], NT, preferred_element_type=F32
                )
        if residual:
            total = total + extra[f].astype(F32).reshape(rows * columns, channels)
        done = total.astype(BF16)
        out[f] = done.reshape(rows, columns, channels)
        if not residual:
            mean, spread = channel_stats(done.astype(F32))
            stats_out[pl.ds(f, 1)] = mean
            stats_out[pl.ds(frames + f, 1)] = spread
        return carry

    lax.fori_loop(0, frames, frame, 0)


def conv(own, prev, edges, stats, gain, bias, weights, extra=None):
    frames, rows, columns, channels = own.shape
    vmem = pl.BlockSpec(memory_space=pltpu.VMEM)
    shapes = [jax.ShapeDtypeStruct(own.shape, BF16)]
    args = [own, prev, *edges, *stats, gain[None], bias[None], *weights]
    specs = [vmem] * 10 + [pl.BlockSpec(memory_space=pl.ANY)] * len(weights)
    if extra is None:
        shapes.append(jax.ShapeDtypeStruct((2 * frames, channels), F32))
    else:
        args.append(extra)
        specs.append(vmem)
    flops = 2 * frames * rows * columns * channels * channels * TAPS
    return pl.pallas_call(
        functools.partial(conv_kernel, len(weights), extra is not None),
        out_shape=shapes,
        in_specs=specs,
        out_specs=[vmem] * len(shapes),
        scratch_shapes=[
            pltpu.VMEM((4, rows + 2, columns, 3 * channels), BF16),
            pltpu.VMEM((channels, TAPS * channels), BF16),
            pltpu.SemaphoreType.DMA((1,)),
        ],
        cost_estimate=pl.CostEstimate(flops=flops, bytes_accessed=9 << 20, transcendentals=1 << 20),
        name="conv",
    )(*args)


def shards(latents, norm1_gain, conv1_weight, conv1_bias, norm2_gain, conv2_weight, conv2_bias):
    weights1 = [whole_weights(conv1_weight)]
    prev = upward(latents, "tm")
    edges = edge_rows(latents)
    stats = share_stats(stats_of(latents))
    hidden, sums = conv(latents, prev, edges, stats, norm1_gain, conv1_bias, weights1)
    weights2 = [whole_weights(conv2_weight)]
    prev = upward(hidden, "tm")
    edges = edge_rows(hidden)
    stats = share_stats(sums)
    return conv(hidden, prev, edges, stats, norm2_gain, conv2_bias, weights2, latents)[0]


HELD = {
    8: (
        ((0, 0, 0),),
        ((1, 0, 0), (2, 0, 0), (3, 0, 0)),
        ((0, 0, 1),),
        ((0, 1, 0),),
        ((1, 0, 1), (2, 0, 1), (3, 0, 1)),
        ((1, 1, 0), (2, 1, 0), (3, 1, 0)),
        ((0, 1, 1), (1, 1, 1)),
        ((2, 1, 1), (3, 1, 1)),
    ),
    5: (
        ((0, 0, 0), (1, 0, 0), (2, 0, 0), (3, 0, 0)),
        ((0, 0, 1), (1, 0, 1), (2, 0, 1), (3, 0, 1)),
        ((0, 1, 0), (1, 1, 0), (2, 1, 0), (3, 1, 0)),
        ((0, 1, 1), (1, 1, 1)),
        ((2, 1, 1), (3, 1, 1)),
    ),
}
BLOCK = 512
NOTE = 16


def own_piece(shard):
    turned = jnp.swapaxes(shard, 1, 2)
    taps, outs, depth = turned.shape
    clip = lax.axis_index("clip")
    start = (0, (clip % 2) * (outs // 2), (clip // 2) * (depth // 2))
    return lax.dynamic_slice(turned, start, (taps, outs // 2, depth // 2))


def diagonal(note):
    blocks = lax.axis_size("tm")
    pairs = [(t * 2 + y, (t + 1) * 2 + 1 - y) for t in range(blocks - 1) for y in range(2)]
    return lax.ppermute(note, ("tm", "tile"), pairs)


def parts_of(value):
    first = value.astype(BF16).astype(F32)
    second = (value - first).astype(BF16).astype(F32)
    return [first, second, value - first - second]


def write_note(note, edge, mean, spread):
    columns, channels = edge.shape
    note[:columns] = edge
    lines = parts_of(mean) + parts_of(spread)
    lines.append(jnp.zeros((NOTE - 6, channels), F32))
    note[columns:] = jnp.concatenate(lines, axis=0).astype(BF16)


def read_note(lines):
    lines = lines.astype(F32)
    mean = lines[0:1] + lines[1:2] + lines[2:3]
    spread = lines[3:4] + lines[4:5] + lines[5:6]
    return mean, spread


def frame_stats(frame):
    rows, columns, channels = frame.shape

    def total(of):
        def body(r, carry):
            value = of(frame[r].astype(F32))
            return carry + jnp.sum(value.reshape(columns // 8, 8, channels), axis=0)

        lines = lax.fori_loop(0, rows, body, jnp.zeros((8, channels), F32))
        return jnp.sum(lines, axis=0, keepdims=True)

    mean = total(lambda x: x) / (rows * columns)

    def squared(x):
        centered = x - mean
        return centered * centered

    return mean, total(squared)


def notes_kernel(x_ref, note_ref):
    frames, rows, columns, channels = x_ref.shape
    at = jnp.where(lax.axis_index("tile") == 0, rows - 1, 0)
    for f in range(frames):
        mean, spread = frame_stats(x_ref.at[f])
        write_note(note_ref.at[f], x_ref[f, at], mean, spread)


def notes_of(block):
    frames, _, columns, channels = block.shape
    return pl.pallas_call(
        notes_kernel,
        out_shape=jax.ShapeDtypeStruct((frames, columns + NOTE, channels), BF16),
        in_specs=[pl.BlockSpec(memory_space=pltpu.VMEM)],
        out_specs=pl.BlockSpec(memory_space=pltpu.VMEM),
        cost_estimate=pl.CostEstimate(flops=1 << 34, bytes_accessed=1 << 10, transcendentals=0),
        name="notes",
    )(block)


def part_kernel(plan, *refs):
    jobs, lo, hi = plan["jobs"], plan["lo"], plan["hi"]
    refs = dict(zip(plan["names"], refs))
    wide, full, sems = refs["wide"], refs["full"], refs["sems"]
    tm, tile, clip = (lax.axis_index(a) for a in ("tm", "tile", "clip"))
    rows, columns, channels = wide.shape[1] - 2, wide.shape[2], full.shape[1]
    cells = float(rows * columns)

    half, core = clip // 2, clip % 2
    copies = []
    for side in range(2):
        for group, names in enumerate(HELD[plan["groups"]]):
            source = refs["w%d" % (side * plan["groups"] + group)]
            high, deep = source.shape[2:]
            for at, (back, dy, dx) in enumerate(names):
                block = (lax.rem(tm + 4 - back, 4) * 2 + (tile ^ dy)) * 2 + (core ^ side)
                place = full.at[
                    :,
                    pl.ds(pl.multiple_of(block * high, high), high),
                    pl.ds(pl.multiple_of((half ^ dx) * deep, 128), deep),
                ]
                piece = source.at[at, pl.ds(lo, hi - lo)]
                copies.append(pltpu.make_async_copy(piece, place, sems.at[len(copies)]))
    slots = plan["slots"]
    count = len(copies)
    early, late = [], []

    def fetch(group, source, place):
        group.append(pltpu.make_async_copy(source, place, sems.at[count + len(early) + len(late)]))
        group[-1].start()

    inner = jnp.where(tile == 0, rows + 1, 0)
    outer = jnp.where(tile == 0, 0, rows + 1)
    fetch(early, refs["vector"], refs["pair"])
    for slot, frame in enumerate(slots):
        ref, at = plan["raw"][frame]
        if len(refs[ref].shape) == 2:
            for r in range(rows):
                line = refs[ref].at[pl.ds(r * columns, columns)]
                fetch(early, line, refs["raw"].at[slot, r + 1])
            near = refs[ref].at[pl.ds(rows * columns, columns + NOTE)]
        else:
            fetch(early, refs[ref].at[at], refs["raw"].at[slot, pl.ds(1, rows)])
            near = refs["other"].at[frame] if frame >= 0 else refs["before"].at[frame + 2]
        fetch(early, near.at[pl.ds(0, columns)], refs["raw"].at[slot, inner])
        fetch(early, near.at[pl.ds(columns, NOTE)], refs["lines"].at[1, slot])
        if frame >= 0:
            lines = refs["note"].at[frame, pl.ds(columns, NOTE)]
            fetch(early, lines, refs["lines"].at[0, slot])
    for copy in copies:
        copy.start()
    for o in jobs:
        if "start" in refs:
            fetch(late, refs["start"].at[o], refs["sum"].at[o])
        if plan["ends"][o] == "final":
            fetch(late, refs["extra"].at[o], refs["rest"].at[o])
    for copy in early:
        copy.wait()

    means, spreads = [[], []], [[], []]
    for slot, frame in enumerate(slots):
        if frame >= 0:
            here = read_note(refs["lines"][0, slot])
        else:
            here = frame_stats(refs["raw"].at[slot, pl.ds(1, rows)])
        there = read_note(refs["lines"][1, slot])
        for side, (mean, spread) in enumerate((here, there)):
            means[side].append(mean)
            spreads[side].append(spread)
    stats = jnp.stack([jnp.concatenate(means[s] + spreads[s], axis=0) for s in range(2)])
    mean_of, scale_of = pool_terms(stats, refs["pair"][0:1], cells)
    for slot in range(len(slots)):
        refs["terms"][slot, 0:1] = mean_of[slot : slot + 1]
        refs["terms"][slot, 1:2] = scale_of[slot : slot + 1] * 0.5
        wide[slot, outer] = jnp.zeros((columns, 3 * channels), BF16)

    column = lax.broadcasted_iota(jnp.int32, (columns, channels), 0)
    halos = sum(frame < 0 for frame in slots)
    shown = rows + 1

    def put(i, carry):
        slot = i // shown
        row = i % shown + jnp.where(tile == 0, 1, 0)
        x = refs["raw"][slot, row].astype(F32)
        half_y = (x - refs["terms"][slot, 0:1]) * refs["terms"][slot, 1:2]
        y = half_y * (1.0 + jnp.tanh(half_y))
        if halos:
            y = jnp.where((slot < halos) & (tm == 0), 0.0, y)
        left = jnp.where(column == 0, 0.0, pltpu.roll(y, 1, 0))
        right = jnp.where(column == columns - 1, 0.0, pltpu.roll(y, columns - 1, 0))
        wide[slot, row, :, :channels] = left.astype(BF16)
        wide[slot, row, :, channels : 2 * channels] = y.astype(BF16)
        wide[slot, row, :, 2 * channels :] = right.astype(BF16)
        return carry

    lax.fori_loop(0, len(slots) * shown, put, 0, unroll=1)

    for copy in copies + late:
        copy.wait()

    step = BLOCK // columns
    leaving = []
    for o, dfs in jobs.items():
        kind = plan["ends"][o]

        def leave(m, o=o):
            here = pl.ds(m * step, step)
            spot = refs["done_at"].at[o, here]
            place = refs["out"].at[plan["spot"].get(o, o), here]
            return pltpu.make_async_copy(spot, place, refs["done_sem"].at[o * rows + m])

        def block(m, carry, o=o, dfs=dfs, kind=kind, leave=leave):
            here = pl.ds(m * step, step)
            flat = pl.ds(pl.multiple_of(m * BLOCK, BLOCK), BLOCK)
            if "start" in refs:
                total = refs["sum"][o, flat]
            else:
                total = jnp.broadcast_to(refs["pair"][1:2], (BLOCK, channels))
            for df in dfs:
                slot = slots.index(o + df - 2)
                for dh in range(3):
                    left = wide[slot, pl.ds(dh + m * step, step)].reshape(BLOCK, 3 * channels)
                    tap = 9 * df + 3 * dh - lo
                    right = jnp.concatenate([full[tap + i] for i in range(3)], axis=1)
                    total = total + lax.dot_general(left, right, NT, preferred_element_type=F32)
            if kind == "partial":
                refs["partial"][o, flat] = total
                return carry
            if kind == "final":
                total = total + refs["rest"][o, here].astype(F32).reshape(BLOCK, channels)
            refs["done_at"][o, here] = total.astype(BF16).reshape(step, columns, channels)
            leave(m).start()
            return carry

        lax.fori_loop(0, rows // step, block, 0)
        if kind == "hidden":
            mean, spread = frame_stats(refs["done_at"].at[o])
            edge = refs["done_at"][o, jnp.where(tile == 0, rows - 1, 0)]
            write_note(refs["new"].at[plan["spot"].get(o, o)], edge, mean, spread)
            if "keep" in refs:
                keep = pltpu.make_async_copy(refs["keep"], refs["new"].at[pl.ds(1, 1)], sems.at[0])
                keep.start()
                keep.wait()
        if kind != "partial":
            leaving += [leave(m) for m in range(rows // step)]
    for copy in leaving:
        copy.wait()


def part_conv(inputs, outputs, jobs, ends, raw, weights, aliases=None, cost=1 << 10, spot={}, **more):
    slots = sorted({o + df - 2 for o, dfs in jobs.items() for df in dfs})
    dfs = sorted({df for group in jobs.values() for df in group})
    lo, hi = 9 * dfs[0], 9 * (dfs[-1] + 1)
    inputs = {**inputs, **{"w%d" % i: w for i, w in enumerate(weights)}}
    _, rows, columns, channels = inputs[next(n for n in ("own", "extra", "own0") if n in inputs)].shape
    plan = dict(spot=spot, groups=len(weights) // 2, jobs=jobs, ends=ends, raw=raw, slots=slots, lo=lo, hi=hi, **more)
    scratch = ["wide", "full", "sems", "raw", "lines", "sum", "rest", "terms", "pair", "done_at", "done_sem"]
    plan["names"] = [*inputs, *outputs, *scratch]
    small = ()
    vmem = pl.BlockSpec(memory_space=pltpu.VMEM)
    anywhere = pl.BlockSpec(memory_space=pl.ANY)
    aliases = aliases or {}
    out_specs = [anywhere if name == "out" else vmem for name in outputs]
    return pl.pallas_call(
        functools.partial(part_kernel, plan),
        out_shape=list(outputs.values()),
        in_specs=[vmem if name in small else anywhere for name in inputs],
        out_specs=out_specs,
        scratch_shapes=[
            pltpu.VMEM((len(slots), rows + 2, columns, 3 * channels), BF16),
            pltpu.VMEM((hi - lo, channels, channels), BF16),
            pltpu.SemaphoreType.DMA((80,)),
            pltpu.VMEM((len(slots), rows + 2, columns, channels), BF16),
            pltpu.VMEM((2, len(slots), NOTE, channels), BF16),
            pltpu.VMEM((2 if "start" in inputs else 1, rows * columns, channels), F32),
            pltpu.VMEM((2, rows, columns, channels), BF16),
            pltpu.VMEM((len(slots), 8, channels), F32),
            pltpu.VMEM((2, channels), F32),
            pltpu.VMEM((2, rows, columns, channels), BF16),
            pltpu.SemaphoreType.DMA((2 * rows,)),
        ],
        input_output_aliases={
            list(inputs).index(source): list(outputs).index(target)
            for source, target in aliases.items()
        },
        cost_estimate=pl.CostEstimate(
            flops=cost,
            bytes_accessed=1 << 10,
            transcendentals=0,
        ),
        name="conv_" + "_".join("%d%s" % (o, "".join(map(str, d))) for o, d in jobs.items()),
    )(*inputs.values())


def along_tm(quarter):
    return [cyclic(quarter, "tm", steps) for steps in (3, 2, 1)][::-1]


def both_cores(arrays):
    return arrays + [swap(a, "clip", 1) for a in arrays]


def hold(*values):
    return lax.optimization_barrier(values)


def shards_fast(
    latents, norm1_gain, conv1_weight, conv1_bias, norm2_gain, conv2_weight, conv2_bias
):
    _, rows, columns, channels = latents.shape
    block = jax.ShapeDtypeStruct(latents.shape, BF16)
    frame = jax.ShapeDtypeStruct((1, rows, columns, channels), BF16)
    note_like = jax.ShapeDtypeStruct((1, columns + NOTE, channels), BF16)
    notes_like = jax.ShapeDtypeStruct((2, columns + NOTE, channels), BF16)
    sums = jax.ShapeDtypeStruct((2, rows * columns, channels), F32)
    vector1 = jnp.stack([norm1_gain, conv1_bias])
    vector2 = jnp.stack([norm2_gain, conv2_bias])

    quarter1, quarter2 = own_piece(conv1_weight)[None], own_piece(conv2_weight)[None]
    turned = along_tm(quarter1)
    near1 = swap(quarter1, "clip", 2), swap(quarter1, "tile", 1)
    quarter1_n, latents_n = hold(quarter1, latents)
    notes = notes_of(latents_n)
    other = swap(notes, "tile", 1)
    turned, near1, other, latents_b = hold(turned, near1, other, latents)

    flat = latents_b.reshape(2, rows * columns, channels)
    send1 = jnp.concatenate([flat[1], other[1]])
    send0 = jnp.concatenate([flat[0], other[0]])
    up1 = upward(send1, "tm")
    held1 = jnp.concatenate(turned)
    far1 = swap(held1, "clip", 2), swap(held1, "tile", 1)
    far1, up1, quarter2 = hold(far1, up1, quarter2)

    corners1 = (
        swap(jnp.concatenate([near1[1], far1[1][:1]]), "clip", 2),
        swap(far1[0][1:], "tile", 1),
    )
    weights1 = both_cores([quarter1, held1, *near1, *far1, *corners1])
    turned2 = along_tm(quarter2)
    turned2, send0 = hold(turned2, send0)
    up0 = upward(send0, "tm")
    held2 = jnp.concatenate([quarter2, *turned2])
    weights1, held2 = hold(weights1, held2)
    far2 = swap(held2, "clip", 2), swap(held2, "tile", 1)
    first = dict(note=notes, other=other, vector=vector1, own=latents)
    hidden1, note1 = part_conv(
        {**first, "odd": up1},
        {"out": frame, "new": note_like},
        {1: (0, 1, 2)},
        {1: "hidden"},
        {-1: ("odd", 0), 0: ("own", 0), 1: ("own", 1)},
        weights1,
        cost=1 << 34,
        spot={1: 0},
    )

    high1 = upward(hidden1, "tm")
    far2, up0 = hold(far2, up0)
    corners2 = swap(far2[1][:2], "clip", 2), swap(far2[0][2:], "tile", 1)
    hidden0, notes_h = part_conv(
        {**first, "odd": up1, "even": up0, "keep": note1},
        {"out": frame, "new": notes_like},
        {0: (0, 1, 2)},
        {0: "hidden"},
        {-2: ("even", 0), -1: ("odd", 0), 0: ("own", 0)},
        weights1,
        cost=1 << 34,
    )

    other_h = swap(notes_h, "tile", 1)
    before_h = diagonal(notes_h)
    hidden0_d = hidden0
    high0 = upward(hidden0_d, "tm")
    corners2, high1 = hold(corners2, high1)
    weights2 = both_cores([held2, *far2, *corners2])
    (partial,) = part_conv(
        dict(note=notes_h, other=other_h, vector=vector2, own0=hidden0, own1=hidden1),
        {"partial": sums},
        {1: (1, 2), 0: (2,)},
        {1: "partial", 0: "partial"},
        {0: ("own0", 0), 1: ("own1", 0)},
        weights2,
        cost=1 << 10,
    )
    (out,) = part_conv(
        dict(
            before=before_h, vector=vector2, odd=high1, even=high0, start=partial, extra=latents
        ),
        {"out": block},
        {1: (0,), 0: (0, 1)},
        {1: "final", 0: "final"},
        {-2: ("even", 0), -1: ("odd", 0)},
        weights2,
    )
    return out


def solution(mesh):
    placed = (
        P(("clip", "tm"), "tile", None, None),
        P(),
        P(None, None, ("tm", "tile")),
        P(),
        P(),
        P(None, None, ("tm", "tile")),
        P(),
    )
    sizes = tuple(mesh.shape[a] for a in ("tm", "tile", "clip"))
    return jax.shard_map(
        shards_fast if sizes == (4, 2, 4) else shards,
        mesh=mesh,
        in_specs=placed,
        out_specs=P(("clip", "tm"), "tile", None, None),
        check_vma=False,
    )
```

```python
import functools

import jax
import jax.numpy as jnp
from jax import lax
from jax.experimental import pallas as pl
from jax.experimental.pallas import tpu as pltpu
from jax.sharding import PartitionSpec as P

GROUPS = 32
TAPS = 27
epsilon = 1e-06
F32 = jnp.float32
BF16 = jnp.bfloat16
NT = (((1,), (1,)), ((), ()))


def upward(value, axis, steps=1):
    count = lax.axis_size(axis)
    first, last = (max(0, -steps), min(count, count - steps))
    return lax.ppermute(value, axis, [(source, source + steps) for source in range(first, last)])


def cyclic(value, axis, steps):
    count = lax.axis_size(axis)
    return lax.ppermute(value, axis, [(i, (i + steps) % count) for i in range(count)])


def swap(value, axis, bit):
    count = lax.axis_size(axis)
    return lax.ppermute(value, axis, [(i, i ^ bit) for i in range(count)])


def edge_rows(block):
    tiles = lax.axis_size("tile")
    if tiles == 2:
        mine = jnp.where(lax.axis_index("tile") == 0, block[:, -1:], block[:, :1])
        own = swap(mine, "tile", 1)
        blocks = lax.axis_size("tm")
        pairs = [(t * 2 + y, (t + 1) * 2 + 1 - y) for t in range(blocks - 1) for y in range(2)]
        before = lax.ppermute(mine, ("tm", "tile"), pairs)
        return own, own, before, before
    low = upward(block[:, -1:], "tile", 1)
    high = upward(block[:, :1], "tile", -1)
    return low, high, upward(low, "tm"), upward(high, "tm")


def share_stats(stats):
    if lax.axis_size("tile") == 2:
        both = jnp.stack([stats, swap(stats, "tile", 1)])
    else:
        both = lax.all_gather(stats, "tile", axis=0)
    return both, upward(both, "tm")


def whole_weights(shard):
    whole = lax.all_gather(shard, ("tm", "tile"), axis=2, tiled=True)
    return whole.reshape(-1, whole.shape[2]).T


def channel_stats(rows):
    mean = jnp.sum(rows, axis=0, keepdims=True) / rows.shape[0]
    centered = rows - mean
    return mean, jnp.sum(centered * centered, axis=0, keepdims=True)


def stats_kernel(x_ref, s_ref):
    frames, rows, columns, channels = x_ref.shape
    for f in range(frames):
        mean, spread = channel_stats(x_ref[f].astype(F32).reshape(rows * columns, channels))
        s_ref[f : f + 1] = mean
        s_ref[frames + f : frames + f + 1] = spread


def stats_of(block):
    frames, _, _, channels = block.shape
    return pl.pallas_call(
        stats_kernel,
        out_shape=jax.ShapeDtypeStruct((2 * frames, channels), F32),
        in_specs=[pl.BlockSpec(memory_space=pltpu.VMEM)],
        out_specs=pl.BlockSpec(memory_space=pltpu.VMEM),
        name="stats",
    )(block)


def norm_terms(stats, gain, cells):
    tiles, twice, channels = stats.shape
    frames = twice // 2
    width = channels // GROUPS
    a = lax.broadcasted_iota(jnp.int32, (channels, channels), 0) // width
    b = lax.broadcasted_iota(jnp.int32, (channels, channels), 1) // width
    same = jnp.where(a == b, 1.0, 0.0).astype(F32)
    pool = functools.partial(jnp.dot, precision=lax.Precision.HIGHEST, preferred_element_type=F32)
    mean = pool(jnp.sum(stats[:, :frames], axis=0), same) / (tiles * width)
    off = stats[:, :frames] - mean[None]
    spread = jnp.sum(stats[:, frames:] + cells * (off * off), axis=0)
    var = pool(spread, same) / (tiles * width * cells)
    return mean, lax.rsqrt(var + epsilon) * gain


def pool_terms(stats, gain, cells):
    tiles, twice, channels = stats.shape
    frames = twice // 2
    width = channels // GROUPS
    a = lax.broadcasted_iota(jnp.int32, (channels, channels), 0) // width
    b = lax.broadcasted_iota(jnp.int32, (channels, channels), 1) // width
    same = jnp.where(a == b, 1.0, 0.0).astype(BF16)

    def pool(value):
        parts = jnp.concatenate(parts_of(value), axis=0).astype(BF16)
        sums = jnp.dot(parts, same, preferred_element_type=F32)
        return sums[:frames] + sums[frames : 2 * frames] + sums[2 * frames :]

    mean = pool(jnp.sum(stats[:, :frames], axis=0)) / (tiles * width)
    off = stats[:, :frames] - mean[None]
    spread = jnp.sum(stats[:, frames:] + cells * (off * off), axis=0)
    var = pool(spread) / (tiles * width * cells)
    return mean, lax.rsqrt(var + epsilon) * gain


def conv_kernel(n_weights, residual, *refs):
    own, prev, low_o, high_o, low_p, high_p, st_o, st_p, gain, bias = refs[:10]
    weights = refs[10 : 10 + n_weights]
    if residual:
        extra, out = refs[10 + n_weights : 12 + n_weights]
        wide, full, sems = refs[12 + n_weights :]
    else:
        out, stats_out = refs[10 + n_weights : 12 + n_weights]
        wide, full, sems = refs[12 + n_weights :]
    frames, rows, columns, channels = own.shape
    span = 3 * channels

    copies = [pltpu.make_async_copy(weights[0], full, sems.at[0])]
    for copy in copies:
        copy.start()

    cells = float(rows * columns)
    here = norm_terms(st_o[...], gain[...], cells)
    before = norm_terms(st_p[...], gain[...], cells)
    first_tile = lax.axis_index("tile") == 0
    last_tile = lax.axis_index("tile") == lax.axis_size("tile") - 1
    start = lax.axis_index("tm") == 0
    column = lax.broadcasted_iota(jnp.int32, (columns, channels), 0)

    def put(slot, row, raw, mean, scale, empty):
        half_y = (raw.astype(F32) - mean) * (0.5 * scale)
        y = half_y * (1.0 + jnp.tanh(half_y))
        if empty is not None:
            y = jnp.where(empty, 0.0, y)
        left = jnp.where(column == 0, 0.0, pltpu.roll(y, 1, 0))
        right = jnp.where(column == columns - 1, 0.0, pltpu.roll(y, columns - 1, 0))
        wide[slot, row, :, :channels] = left.astype(BF16)
        wide[slot, row, :, channels : 2 * channels] = y.astype(BF16)
        wide[slot, row, :, 2 * channels :] = right.astype(BF16)

    for f in range(2):
        mean, scale = here[0][f : f + 1], here[1][f : f + 1]

        def body(r, carry, f=f, mean=mean, scale=scale):
            put(2 + f, r + 1, own[f, r], mean, scale, None)
            return carry

        lax.fori_loop(0, rows, body, 0)
        put(2 + f, 0, low_o[f, 0], mean, scale, first_tile)
        put(2 + f, rows + 1, high_o[f, 0], mean, scale, last_tile)
    for f in range(2):
        mean, scale = before[0][f : f + 1], before[1][f : f + 1]

        def body(r, carry, f=f, mean=mean, scale=scale):
            put(f, r + 1, prev[f, r], mean, scale, start)
            return carry

        lax.fori_loop(0, rows, body, 0)
        put(f, 0, low_p[f, 0], mean, scale, start | first_tile)
        put(f, rows + 1, high_p[f, 0], mean, scale, start | last_tile)

    for copy in copies:
        copy.wait()

    def frame(f, carry):
        total = jnp.broadcast_to(bias[...], (rows * columns, channels))
        for df in range(3):
            for dh in range(3):
                left = wide[f + df, dh : dh + rows].reshape(rows * columns, span)
                at = (3 * df + dh) * span
                total = total + lax.dot_general(
                    left, full[:, at : at + span], NT, preferred_element_type=F32
                )
        if residual:
            total = total + extra[f].astype(F32).reshape(rows * columns, channels)
        done = total.astype(BF16)
        out[f] = done.reshape(rows, columns, channels)
        if not residual:
            mean, spread = channel_stats(done.astype(F32))
            stats_out[pl.ds(f, 1)] = mean
            stats_out[pl.ds(frames + f, 1)] = spread
        return carry

    lax.fori_loop(0, frames, frame, 0)


def conv(own, prev, edges, stats, gain, bias, weights, extra=None):
    frames, rows, columns, channels = own.shape
    vmem = pl.BlockSpec(memory_space=pltpu.VMEM)
    shapes = [jax.ShapeDtypeStruct(own.shape, BF16)]
    args = [own, prev, *edges, *stats, gain[None], bias[None], *weights]
    specs = [vmem] * 10 + [pl.BlockSpec(memory_space=pl.ANY)] * len(weights)
    if extra is None:
        shapes.append(jax.ShapeDtypeStruct((2 * frames, channels), F32))
    else:
        args.append(extra)
        specs.append(vmem)
    flops = 2 * frames * rows * columns * channels * channels * TAPS
    return pl.pallas_call(
        functools.partial(conv_kernel, len(weights), extra is not None),
        out_shape=shapes,
        in_specs=specs,
        out_specs=[vmem] * len(shapes),
        scratch_shapes=[
            pltpu.VMEM((4, rows + 2, columns, 3 * channels), BF16),
            pltpu.VMEM((channels, TAPS * channels), BF16),
            pltpu.SemaphoreType.DMA((1,)),
        ],
        cost_estimate=pl.CostEstimate(flops=flops, bytes_accessed=9 << 20, transcendentals=1 << 20),
        name="conv",
    )(*args)


def shards(latents, norm1_gain, conv1_weight, conv1_bias, norm2_gain, conv2_weight, conv2_bias):
    weights1 = [whole_weights(conv1_weight)]
    prev = upward(latents, "tm")
    edges = edge_rows(latents)
    stats = share_stats(stats_of(latents))
    hidden, sums = conv(latents, prev, edges, stats, norm1_gain, conv1_bias, weights1)
    weights2 = [whole_weights(conv2_weight)]
    prev = upward(hidden, "tm")
    edges = edge_rows(hidden)
    stats = share_stats(sums)
    return conv(hidden, prev, edges, stats, norm2_gain, conv2_bias, weights2, latents)[0]


HELD = {
    8: (
        ((0, 0, 0),),
        ((1, 0, 0), (2, 0, 0), (3, 0, 0)),
        ((0, 0, 1),),
        ((0, 1, 0),),
        ((1, 0, 1), (2, 0, 1), (3, 0, 1)),
        ((1, 1, 0), (2, 1, 0), (3, 1, 0)),
        ((0, 1, 1), (1, 1, 1)),
        ((2, 1, 1), (3, 1, 1)),
    ),
    5: (
        ((0, 0, 0), (1, 0, 0), (2, 0, 0), (3, 0, 0)),
        ((0, 0, 1), (1, 0, 1), (2, 0, 1), (3, 0, 1)),
        ((0, 1, 0), (1, 1, 0), (2, 1, 0), (3, 1, 0)),
        ((0, 1, 1), (1, 1, 1)),
        ((2, 1, 1), (3, 1, 1)),
    ),
}
BLOCK = 512
NOTE = 16


def own_piece(shard):
    turned = jnp.swapaxes(shard, 1, 2)
    taps, outs, depth = turned.shape
    clip = lax.axis_index("clip")
    start = (0, (clip % 2) * (outs // 2), (clip // 2) * (depth // 2))
    return lax.dynamic_slice(turned, start, (taps, outs // 2, depth // 2))


def diagonal(note):
    blocks = lax.axis_size("tm")
    pairs = [(t * 2 + y, (t + 1) * 2 + 1 - y) for t in range(blocks - 1) for y in range(2)]
    return lax.ppermute(note, ("tm", "tile"), pairs)


def parts_of(value):
    first = value.astype(BF16).astype(F32)
    second = (value - first).astype(BF16).astype(F32)
    return [first, second, value - first - second]


def write_note(note, edge, mean, spread):
    columns, channels = edge.shape
    note[:columns] = edge
    lines = parts_of(mean) + parts_of(spread)
    lines.append(jnp.zeros((NOTE - 6, channels), F32))
    note[columns:] = jnp.concatenate(lines, axis=0).astype(BF16)


def read_note(lines):
    lines = lines.astype(F32)
    mean = lines[0:1] + lines[1:2] + lines[2:3]
    spread = lines[3:4] + lines[4:5] + lines[5:6]
    return mean, spread


def frame_stats(frame):
    rows, columns, channels = frame.shape

    def total(of):
        def body(r, carry):
            value = of(frame[r].astype(F32))
            return carry + jnp.sum(value.reshape(columns // 8, 8, channels), axis=0)

        lines = lax.fori_loop(0, rows, body, jnp.zeros((8, channels), F32))
        return jnp.sum(lines, axis=0, keepdims=True)

    mean = total(lambda x: x) / (rows * columns)

    def squared(x):
        centered = x - mean
        return centered * centered

    return mean, total(squared)


def notes_kernel(x_ref, note_ref):
    frames, rows, columns, channels = x_ref.shape
    at = jnp.where(lax.axis_index("tile") == 0, rows - 1, 0)
    for f in range(frames):
        mean, spread = frame_stats(x_ref.at[f])
        write_note(note_ref.at[f], x_ref[f, at], mean, spread)


def notes_of(block):
    frames, _, columns, channels = block.shape
    return pl.pallas_call(
        notes_kernel,
        out_shape=jax.ShapeDtypeStruct((frames, columns + NOTE, channels), BF16),
        in_specs=[pl.BlockSpec(memory_space=pltpu.VMEM)],
        out_specs=pl.BlockSpec(memory_space=pltpu.VMEM),
        cost_estimate=pl.CostEstimate(flops=1 << 34, bytes_accessed=1 << 10, transcendentals=0),
        name="notes",
    )(block)


def part_kernel(plan, *refs):
    jobs, lo, hi = plan["jobs"], plan["lo"], plan["hi"]
    refs = dict(zip(plan["names"], refs))
    wide, full, sems = refs["wide"], refs["full"], refs["sems"]
    tm, tile, clip = (lax.axis_index(a) for a in ("tm", "tile", "clip"))
    rows, columns, channels = wide.shape[1] - 2, wide.shape[2], full.shape[1]
    cells = float(rows * columns)

    half, core = clip // 2, clip % 2
    copies = []
    for side in range(2):
        for group, names in enumerate(HELD[plan["groups"]]):
            source = refs["w%d" % (side * plan["groups"] + group)]
            high, deep = source.shape[2:]
            for at, (back, dy, dx) in enumerate(names):
                block = (lax.rem(tm + 4 - back, 4) * 2 + (tile ^ dy)) * 2 + (core ^ side)
                place = full.at[
                    :,
                    pl.ds(pl.multiple_of(block * high, high), high),
                    pl.ds(pl.multiple_of((half ^ dx) * deep, 128), deep),
                ]
                piece = source.at[at, pl.ds(lo, hi - lo)]
                copies.append(pltpu.make_async_copy(piece, place, sems.at[len(copies)]))
    slots = plan["slots"]
    count = len(copies)
    early, late = [], []

    def fetch(group, source, place):
        group.append(pltpu.make_async_copy(source, place, sems.at[count + len(early) + len(late)]))
        group[-1].start()

    inner = jnp.where(tile == 0, rows + 1, 0)
    outer = jnp.where(tile == 0, 0, rows + 1)
    fetch(early, refs["vector"], refs["pair"])
    for slot, frame in enumerate(slots):
        ref, at = plan["raw"][frame]
        if len(refs[ref].shape) == 2:
            for r in range(rows):
                line = refs[ref].at[pl.ds(r * columns, columns)]
                fetch(early, line, refs["raw"].at[slot, r + 1])
            near = refs[ref].at[pl.ds(rows * columns, columns + NOTE)]
        else:
            fetch(early, refs[ref].at[at], refs["raw"].at[slot, pl.ds(1, rows)])
            near = refs["other"].at[frame] if frame >= 0 else refs["before"].at[frame + 2]
        fetch(early, near.at[pl.ds(0, columns)], refs["raw"].at[slot, inner])
        fetch(early, near.at[pl.ds(columns, NOTE)], refs["lines"].at[1, slot])
        if frame >= 0:
            lines = refs["note"].at[frame, pl.ds(columns, NOTE)]
            fetch(early, lines, refs["lines"].at[0, slot])
    for copy in copies:
        copy.start()
    for o in jobs:
        if "start" in refs:
            fetch(late, refs["start"].at[o], refs["sum"].at[o])
        if plan["ends"][o] == "final":
            fetch(late, refs["extra"].at[o], refs["rest"].at[o])
    for copy in early:
        copy.wait()

    means, spreads = [[], []], [[], []]
    for slot, frame in enumerate(slots):
        if frame >= 0:
            here = read_note(refs["lines"][0, slot])
        else:
            here = frame_stats(refs["raw"].at[slot, pl.ds(1, rows)])
        there = read_note(refs["lines"][1, slot])
        for side, (mean, spread) in enumerate((here, there)):
            means[side].append(mean)
            spreads[side].append(spread)
    stats = jnp.stack([jnp.concatenate(means[s] + spreads[s], axis=0) for s in range(2)])
    mean_of, scale_of = pool_terms(stats, refs["pair"][0:1], cells)
    for slot in range(len(slots)):
        refs["terms"][slot, 0:1] = mean_of[slot : slot + 1]
        refs["terms"][slot, 1:2] = scale_of[slot : slot + 1] * 0.5
        wide[slot, outer] = jnp.zeros((columns, 3 * channels), BF16)

    column = lax.broadcasted_iota(jnp.int32, (columns, channels), 0)
    halos = sum(frame < 0 for frame in slots)
    shown = rows + 1

    def put(i, carry):
        slot = i // shown
        row = i % shown + jnp.where(tile == 0, 1, 0)
        x = refs["raw"][slot, row].astype(F32)
        half_y = (x - refs["terms"][slot, 0:1]) * refs["terms"][slot, 1:2]
        y = half_y * (1.0 + jnp.tanh(half_y))
        if halos:
            y = jnp.where((slot < halos) & (tm == 0), 0.0, y)
        left = jnp.where(column == 0, 0.0, pltpu.roll(y, 1, 0))
        right = jnp.where(column == columns - 1, 0.0, pltpu.roll(y, columns - 1, 0))
        wide[slot, row, :, :channels] = left.astype(BF16)
        wide[slot, row, :, channels : 2 * channels] = y.astype(BF16)
        wide[slot, row, :, 2 * channels :] = right.astype(BF16)
        return carry

    lax.fori_loop(0, len(slots) * shown, put, 0, unroll=3)

    for copy in copies:
        copy.wait()

    step = BLOCK // columns
    leaving = []
    for o, dfs in jobs.items():
        kind = plan["ends"][o]

        def leave(m, o=o):
            here = pl.ds(m * step, step)
            spot = refs["done_at"].at[o, here]
            place = refs["out"].at[plan["spot"].get(o, o), here]
            return pltpu.make_async_copy(spot, place, refs["done_sem"].at[o * rows + m])

        def block(m, carry, o=o, dfs=dfs, kind=kind, leave=leave):
            here = pl.ds(m * step, step)
            flat = pl.ds(pl.multiple_of(m * BLOCK, BLOCK), BLOCK)
            total = None if "start" in refs else jnp.broadcast_to(
                refs["pair"][1:2], (BLOCK, channels)
            )
            for df in dfs:
                slot = slots.index(o + df - 2)
                for dh in range(3):
                    left = wide[slot, pl.ds(dh + m * step, step)].reshape(BLOCK, 3 * channels)
                    tap = 9 * df + 3 * dh - lo
                    right = jnp.concatenate([full[tap + i] for i in range(3)], axis=1)
                    part = lax.dot_general(left, right, NT, preferred_element_type=F32)
                    total = part if total is None else total + part
            if late and o == list(jobs)[0]:

                @pl.when(m == 0)
                def _():
                    for copy in late:
                        copy.wait()

            if "start" in refs:
                total = total + refs["sum"][o, flat]
            if kind == "partial":
                refs["partial"][o, flat] = total
                return carry
            if kind == "final":
                total = total + refs["rest"][o, here].astype(F32).reshape(BLOCK, channels)
            refs["done_at"][o, here] = total.astype(BF16).reshape(step, columns, channels)
            leave(m).start()
            return carry

        lax.fori_loop(0, rows // step, block, 0)
        if kind == "hidden":
            mean, spread = frame_stats(refs["done_at"].at[o])
            edge = refs["done_at"][o, jnp.where(tile == 0, rows - 1, 0)]
            write_note(refs["new"].at[plan["spot"].get(o, o)], edge, mean, spread)
            if "keep" in refs:
                keep = pltpu.make_async_copy(refs["keep"], refs["new"].at[pl.ds(1, 1)], sems.at[0])
                keep.start()
                keep.wait()
        if kind != "partial":
            leaving += [leave(m) for m in range(rows // step)]
    for copy in leaving:
        copy.wait()


def part_conv(inputs, outputs, jobs, ends, raw, weights, aliases=None, cost=1 << 10, spot={}, **more):
    slots = sorted({o + df - 2 for o, dfs in jobs.items() for df in dfs})
    dfs = sorted({df for group in jobs.values() for df in group})
    lo, hi = 9 * dfs[0], 9 * (dfs[-1] + 1)
    inputs = {**inputs, **{"w%d" % i: w for i, w in enumerate(weights)}}
    _, rows, columns, channels = inputs[next(n for n in ("own", "extra", "own0") if n in inputs)].shape
    plan = dict(spot=spot, groups=len(weights) // 2, jobs=jobs, ends=ends, raw=raw, slots=slots, lo=lo, hi=hi, **more)
    scratch = ["wide", "full", "sems", "raw", "lines", "sum", "rest", "terms", "pair", "done_at", "done_sem"]
    plan["names"] = [*inputs, *outputs, *scratch]
    small = ()
    vmem = pl.BlockSpec(memory_space=pltpu.VMEM)
    anywhere = pl.BlockSpec(memory_space=pl.ANY)
    aliases = aliases or {}
    out_specs = [anywhere if name == "out" else vmem for name in outputs]
    return pl.pallas_call(
        functools.partial(part_kernel, plan),
        out_shape=list(outputs.values()),
        in_specs=[vmem if name in small else anywhere for name in inputs],
        out_specs=out_specs,
        scratch_shapes=[
            pltpu.VMEM((len(slots), rows + 2, columns, 3 * channels), BF16),
            pltpu.VMEM((hi - lo, channels, channels), BF16),
            pltpu.SemaphoreType.DMA((80,)),
            pltpu.VMEM((len(slots), rows + 2, columns, channels), BF16),
            pltpu.VMEM((2, len(slots), NOTE, channels), BF16),
            pltpu.VMEM((2 if "start" in inputs else 1, rows * columns, channels), F32),
            pltpu.VMEM((2, rows, columns, channels), BF16),
            pltpu.VMEM((len(slots), 8, channels), F32),
            pltpu.VMEM((2, channels), F32),
            pltpu.VMEM((2, rows, columns, channels), BF16),
            pltpu.SemaphoreType.DMA((2 * rows,)),
        ],
        input_output_aliases={
            list(inputs).index(source): list(outputs).index(target)
            for source, target in aliases.items()
        },
        cost_estimate=pl.CostEstimate(
            flops=cost,
            bytes_accessed=1 << 10,
            transcendentals=0,
        ),
        name="conv_" + "_".join("%d%s" % (o, "".join(map(str, d))) for o, d in jobs.items()),
    )(*inputs.values())


def along_tm(quarter):
    return [cyclic(quarter, "tm", steps) for steps in (3, 2, 1)][::-1]


def both_cores(arrays):
    return arrays + [swap(a, "clip", 1) for a in arrays]


def hold(*values):
    return lax.optimization_barrier(values)


def shards_fast(
    latents, norm1_gain, conv1_weight, conv1_bias, norm2_gain, conv2_weight, conv2_bias
):
    _, rows, columns, channels = latents.shape
    block = jax.ShapeDtypeStruct(latents.shape, BF16)
    frame = jax.ShapeDtypeStruct((1, rows, columns, channels), BF16)
    note_like = jax.ShapeDtypeStruct((1, columns + NOTE, channels), BF16)
    notes_like = jax.ShapeDtypeStruct((2, columns + NOTE, channels), BF16)
    vector1 = jnp.stack([norm1_gain, conv1_bias])
    vector2 = jnp.stack([norm2_gain, conv2_bias])

    quarter1, quarter2 = own_piece(conv1_weight)[None], own_piece(conv2_weight)[None]
    turned = along_tm(quarter1)
    near1 = swap(quarter1, "clip", 2), swap(quarter1, "tile", 1)
    quarter1_n, latents_n = hold(quarter1, latents)
    notes = notes_of(latents_n)
    other = swap(notes, "tile", 1)
    turned, near1, other, latents_b = hold(turned, near1, other, latents)

    flat = latents_b.reshape(2, rows * columns, channels)
    send1 = jnp.concatenate([flat[1], other[1]])
    send0 = jnp.concatenate([flat[0], other[0]])
    up1 = upward(send1, "tm")
    held1 = jnp.concatenate(turned)
    far1 = swap(held1, "clip", 2), swap(held1, "tile", 1)
    far1, up1, quarter2 = hold(far1, up1, quarter2)

    corners1 = (
        swap(jnp.concatenate([near1[1], far1[1][:1]]), "clip", 2),
        swap(far1[0][1:], "tile", 1),
    )
    weights1 = both_cores([quarter1, held1, *near1, *far1, *corners1])
    turned2 = along_tm(quarter2)
    turned2, send0 = hold(turned2, send0)
    up0 = upward(send0, "tm")
    held2 = jnp.concatenate([quarter2, *turned2])
    weights1, held2 = hold(weights1, held2)
    far2 = swap(held2, "clip", 2), swap(held2, "tile", 1)
    first = dict(note=notes, other=other, vector=vector1, own=latents)
    hidden1, note1 = part_conv(
        {**first, "odd": up1},
        {"out": frame, "new": note_like},
        {1: (0, 1, 2)},
        {1: "hidden"},
        {-1: ("odd", 0), 0: ("own", 0), 1: ("own", 1)},
        weights1,
        cost=1 << 34,
        spot={1: 0},
    )

    high1 = upward(hidden1, "tm")
    far2, up0 = hold(far2, up0)
    corners2 = swap(far2[1][:2], "clip", 2), swap(far2[0][2:], "tile", 1)
    hidden0, notes_h = part_conv(
        {**first, "odd": up1, "even": up0, "keep": note1},
        {"out": frame, "new": notes_like},
        {0: (0, 1, 2)},
        {0: "hidden"},
        {-2: ("even", 0), -1: ("odd", 0), 0: ("own", 0)},
        weights1,
        cost=1 << 34,
    )

    other_h = swap(notes_h, "tile", 1)
    before_h = diagonal(notes_h)
    hidden0_d = hidden0
    high0 = upward(hidden0_d, "tm")
    weights2 = both_cores([held2, *far2, *corners2])
    (out,) = part_conv(
        dict(
            note=notes_h, other=other_h, before=before_h, vector=vector2, own0=hidden0,
            own1=hidden1, odd=high1, even=high0, extra=latents,
        ),
        {"out": block},
        {1: (0, 1, 2), 0: (0, 1, 2)},
        {1: "final", 0: "final"},
        {-2: ("even", 0), -1: ("odd", 0), 0: ("own0", 0), 1: ("own1", 0)},
        weights2,
    )
    return out


def solution(mesh):
    placed = (
        P(("clip", "tm"), "tile", None, None),
        P(),
        P(None, None, ("tm", "tile")),
        P(),
        P(),
        P(None, None, ("tm", "tile")),
        P(),
    )
    sizes = tuple(mesh.shape[a] for a in ("tm", "tile", "clip"))
    return jax.shard_map(
        shards_fast if sizes == (4, 2, 4) else shards,
        mesh=mesh,
        in_specs=placed,
        out_specs=P(("clip", "tm"), "tile", None, None),
        check_vma=False,
    )
```

```python
import functools

import jax
import jax.numpy as jnp
from jax import lax
from jax.experimental import pallas as pl
from jax.experimental.pallas import tpu as pltpu
from jax.sharding import PartitionSpec as P

GROUPS = 32
TAPS = 27
epsilon = 1e-06
F32 = jnp.float32
BF16 = jnp.bfloat16
NT = (((1,), (1,)), ((), ()))


def upward(value, axis, steps=1):
    count = lax.axis_size(axis)
    first, last = (max(0, -steps), min(count, count - steps))
    return lax.ppermute(value, axis, [(source, source + steps) for source in range(first, last)])


def cyclic(value, axis, steps):
    count = lax.axis_size(axis)
    return lax.ppermute(value, axis, [(i, (i + steps) % count) for i in range(count)])


def swap(value, axis, bit):
    count = lax.axis_size(axis)
    return lax.ppermute(value, axis, [(i, i ^ bit) for i in range(count)])


def edge_rows(block):
    tiles = lax.axis_size("tile")
    if tiles == 2:
        mine = jnp.where(lax.axis_index("tile") == 0, block[:, -1:], block[:, :1])
        own = swap(mine, "tile", 1)
        blocks = lax.axis_size("tm")
        pairs = [(t * 2 + y, (t + 1) * 2 + 1 - y) for t in range(blocks - 1) for y in range(2)]
        before = lax.ppermute(mine, ("tm", "tile"), pairs)
        return own, own, before, before
    low = upward(block[:, -1:], "tile", 1)
    high = upward(block[:, :1], "tile", -1)
    return low, high, upward(low, "tm"), upward(high, "tm")


def share_stats(stats):
    if lax.axis_size("tile") == 2:
        both = jnp.stack([stats, swap(stats, "tile", 1)])
    else:
        both = lax.all_gather(stats, "tile", axis=0)
    return both, upward(both, "tm")


def whole_weights(shard):
    whole = lax.all_gather(shard, ("tm", "tile"), axis=2, tiled=True)
    return whole.reshape(-1, whole.shape[2]).T


def channel_stats(rows):
    mean = jnp.sum(rows, axis=0, keepdims=True) / rows.shape[0]
    centered = rows - mean
    return mean, jnp.sum(centered * centered, axis=0, keepdims=True)


def stats_kernel(x_ref, s_ref):
    frames, rows, columns, channels = x_ref.shape
    for f in range(frames):
        mean, spread = channel_stats(x_ref[f].astype(F32).reshape(rows * columns, channels))
        s_ref[f : f + 1] = mean
        s_ref[frames + f : frames + f + 1] = spread


def stats_of(block):
    frames, _, _, channels = block.shape
    return pl.pallas_call(
        stats_kernel,
        out_shape=jax.ShapeDtypeStruct((2 * frames, channels), F32),
        in_specs=[pl.BlockSpec(memory_space=pltpu.VMEM)],
        out_specs=pl.BlockSpec(memory_space=pltpu.VMEM),
        name="stats",
    )(block)


def norm_terms(stats, gain, cells):
    tiles, twice, channels = stats.shape
    frames = twice // 2
    width = channels // GROUPS
    a = lax.broadcasted_iota(jnp.int32, (channels, channels), 0) // width
    b = lax.broadcasted_iota(jnp.int32, (channels, channels), 1) // width
    same = jnp.where(a == b, 1.0, 0.0).astype(F32)
    pool = functools.partial(jnp.dot, precision=lax.Precision.HIGHEST, preferred_element_type=F32)
    mean = pool(jnp.sum(stats[:, :frames], axis=0), same) / (tiles * width)
    off = stats[:, :frames] - mean[None]
    spread = jnp.sum(stats[:, frames:] + cells * (off * off), axis=0)
    var = pool(spread, same) / (tiles * width * cells)
    return mean, lax.rsqrt(var + epsilon) * gain


def pool_terms(stats, gain, cells):
    tiles, twice, channels = stats.shape
    frames = twice // 2
    width = channels // GROUPS
    a = lax.broadcasted_iota(jnp.int32, (channels, channels), 0) // width
    b = lax.broadcasted_iota(jnp.int32, (channels, channels), 1) // width
    same = jnp.where(a == b, 1.0, 0.0).astype(BF16)

    def pool(value):
        parts = jnp.concatenate(parts_of(value), axis=0).astype(BF16)
        sums = jnp.dot(parts, same, preferred_element_type=F32)
        return sums[:frames] + sums[frames : 2 * frames] + sums[2 * frames :]

    mean = pool(jnp.sum(stats[:, :frames], axis=0)) / (tiles * width)
    off = stats[:, :frames] - mean[None]
    spread = jnp.sum(stats[:, frames:] + cells * (off * off), axis=0)
    var = pool(spread) / (tiles * width * cells)
    return mean, lax.rsqrt(var + epsilon) * gain


def conv_kernel(n_weights, residual, *refs):
    own, prev, low_o, high_o, low_p, high_p, st_o, st_p, gain, bias = refs[:10]
    weights = refs[10 : 10 + n_weights]
    if residual:
        extra, out = refs[10 + n_weights : 12 + n_weights]
        wide, full, sems = refs[12 + n_weights :]
    else:
        out, stats_out = refs[10 + n_weights : 12 + n_weights]
        wide, full, sems = refs[12 + n_weights :]
    frames, rows, columns, channels = own.shape
    span = 3 * channels

    copies = [pltpu.make_async_copy(weights[0], full, sems.at[0])]
    for copy in copies:
        copy.start()

    cells = float(rows * columns)
    here = norm_terms(st_o[...], gain[...], cells)
    before = norm_terms(st_p[...], gain[...], cells)
    first_tile = lax.axis_index("tile") == 0
    last_tile = lax.axis_index("tile") == lax.axis_size("tile") - 1
    start = lax.axis_index("tm") == 0
    column = lax.broadcasted_iota(jnp.int32, (columns, channels), 0)

    def put(slot, row, raw, mean, scale, empty):
        half_y = (raw.astype(F32) - mean) * (0.5 * scale)
        y = half_y * (1.0 + jnp.tanh(half_y))
        if empty is not None:
            y = jnp.where(empty, 0.0, y)
        left = jnp.where(column == 0, 0.0, pltpu.roll(y, 1, 0))
        right = jnp.where(column == columns - 1, 0.0, pltpu.roll(y, columns - 1, 0))
        wide[slot, row, :, :channels] = left.astype(BF16)
        wide[slot, row, :, channels : 2 * channels] = y.astype(BF16)
        wide[slot, row, :, 2 * channels :] = right.astype(BF16)

    for f in range(2):
        mean, scale = here[0][f : f + 1], here[1][f : f + 1]

        def body(r, carry, f=f, mean=mean, scale=scale):
            put(2 + f, r + 1, own[f, r], mean, scale, None)
            return carry

        lax.fori_loop(0, rows, body, 0)
        put(2 + f, 0, low_o[f, 0], mean, scale, first_tile)
        put(2 + f, rows + 1, high_o[f, 0], mean, scale, last_tile)
    for f in range(2):
        mean, scale = before[0][f : f + 1], before[1][f : f + 1]

        def body(r, carry, f=f, mean=mean, scale=scale):
            put(f, r + 1, prev[f, r], mean, scale, start)
            return carry

        lax.fori_loop(0, rows, body, 0)
        put(f, 0, low_p[f, 0], mean, scale, start | first_tile)
        put(f, rows + 1, high_p[f, 0], mean, scale, start | last_tile)

    for copy in copies:
        copy.wait()

    def frame(f, carry):
        total = jnp.broadcast_to(bias[...], (rows * columns, channels))
        for df in range(3):
            for dh in range(3):
                left = wide[f + df, dh : dh + rows].reshape(rows * columns, span)
                at = (3 * df + dh) * span
                total = total + lax.dot_general(
                    left, full[:, at : at + span], NT, preferred_element_type=F32
                )
        if residual:
            total = total + extra[f].astype(F32).reshape(rows * columns, channels)
        done = total.astype(BF16)
        out[f] = done.reshape(rows, columns, channels)
        if not residual:
            mean, spread = channel_stats(done.astype(F32))
            stats_out[pl.ds(f, 1)] = mean
            stats_out[pl.ds(frames + f, 1)] = spread
        return carry

    lax.fori_loop(0, frames, frame, 0)


def conv(own, prev, edges, stats, gain, bias, weights, extra=None):
    frames, rows, columns, channels = own.shape
    vmem = pl.BlockSpec(memory_space=pltpu.VMEM)
    shapes = [jax.ShapeDtypeStruct(own.shape, BF16)]
    args = [own, prev, *edges, *stats, gain[None], bias[None], *weights]
    specs = [vmem] * 10 + [pl.BlockSpec(memory_space=pl.ANY)] * len(weights)
    if extra is None:
        shapes.append(jax.ShapeDtypeStruct((2 * frames, channels), F32))
    else:
        args.append(extra)
        specs.append(vmem)
    flops = 2 * frames * rows * columns * channels * channels * TAPS
    return pl.pallas_call(
        functools.partial(conv_kernel, len(weights), extra is not None),
        out_shape=shapes,
        in_specs=specs,
        out_specs=[vmem] * len(shapes),
        scratch_shapes=[
            pltpu.VMEM((4, rows + 2, columns, 3 * channels), BF16),
            pltpu.VMEM((channels, TAPS * channels), BF16),
            pltpu.SemaphoreType.DMA((1,)),
        ],
        cost_estimate=pl.CostEstimate(flops=flops, bytes_accessed=9 << 20, transcendentals=1 << 20),
        name="conv",
    )(*args)


def shards(latents, norm1_gain, conv1_weight, conv1_bias, norm2_gain, conv2_weight, conv2_bias):
    weights1 = [whole_weights(conv1_weight)]
    prev = upward(latents, "tm")
    edges = edge_rows(latents)
    stats = share_stats(stats_of(latents))
    hidden, sums = conv(latents, prev, edges, stats, norm1_gain, conv1_bias, weights1)
    weights2 = [whole_weights(conv2_weight)]
    prev = upward(hidden, "tm")
    edges = edge_rows(hidden)
    stats = share_stats(sums)
    return conv(hidden, prev, edges, stats, norm2_gain, conv2_bias, weights2, latents)[0]


HELD = {
    8: (
        ((0, 0, 0),),
        ((1, 0, 0), (2, 0, 0), (3, 0, 0)),
        ((0, 0, 1),),
        ((0, 1, 0),),
        ((1, 0, 1), (2, 0, 1), (3, 0, 1)),
        ((1, 1, 0), (2, 1, 0), (3, 1, 0)),
        ((0, 1, 1), (1, 1, 1)),
        ((2, 1, 1), (3, 1, 1)),
    ),
    5: (
        ((0, 0, 0), (1, 0, 0), (2, 0, 0), (3, 0, 0)),
        ((0, 0, 1), (1, 0, 1), (2, 0, 1), (3, 0, 1)),
        ((0, 1, 0), (1, 1, 0), (2, 1, 0), (3, 1, 0)),
        ((0, 1, 1), (1, 1, 1)),
        ((2, 1, 1), (3, 1, 1)),
    ),
}
BLOCK = 512
NOTE = 16


def own_piece(shard):
    turned = jnp.swapaxes(shard, 1, 2)
    taps, outs, depth = turned.shape
    clip = lax.axis_index("clip")
    start = (0, (clip % 2) * (outs // 2), (clip // 2) * (depth // 2))
    return lax.dynamic_slice(turned, start, (taps, outs // 2, depth // 2))


def diagonal(note):
    blocks = lax.axis_size("tm")
    pairs = [(t * 2 + y, (t + 1) * 2 + 1 - y) for t in range(blocks - 1) for y in range(2)]
    return lax.ppermute(note, ("tm", "tile"), pairs)


def parts_of(value):
    first = value.astype(BF16).astype(F32)
    second = (value - first).astype(BF16).astype(F32)
    return [first, second, value - first - second]


def write_note(note, edge, mean, spread):
    columns, channels = edge.shape
    note[:columns] = edge
    lines = parts_of(mean) + parts_of(spread)
    lines.append(jnp.zeros((NOTE - 6, channels), F32))
    note[columns:] = jnp.concatenate(lines, axis=0).astype(BF16)


def read_note(lines):
    lines = lines.astype(F32)
    mean = lines[0:1] + lines[1:2] + lines[2:3]
    spread = lines[3:4] + lines[4:5] + lines[5:6]
    return mean, spread


def frame_stats(frame):
    rows, columns, channels = frame.shape

    def total(of):
        def body(r, carry):
            value = of(frame[r].astype(F32))
            return carry + jnp.sum(value.reshape(columns // 8, 8, channels), axis=0)

        lines = lax.fori_loop(0, rows, body, jnp.zeros((8, channels), F32), unroll=8)
        return jnp.sum(lines, axis=0, keepdims=True)

    mean = total(lambda x: x) / (rows * columns)

    def squared(x):
        centered = x - mean
        return centered * centered

    return mean, total(squared)


def notes_kernel(x_ref, note_ref):
    frames, rows, columns, channels = x_ref.shape
    at = jnp.where(lax.axis_index("tile") == 0, rows - 1, 0)
    for f in range(frames):
        mean, spread = frame_stats(x_ref.at[f])
        write_note(note_ref.at[f], x_ref[f, at], mean, spread)


def notes_of(block):
    frames, _, columns, channels = block.shape
    return pl.pallas_call(
        notes_kernel,
        out_shape=jax.ShapeDtypeStruct((frames, columns + NOTE, channels), BF16),
        in_specs=[pl.BlockSpec(memory_space=pltpu.VMEM)],
        out_specs=pl.BlockSpec(memory_space=pltpu.VMEM),
        cost_estimate=pl.CostEstimate(flops=1 << 34, bytes_accessed=1 << 10, transcendentals=0),
        name="notes",
    )(block)


def part_kernel(plan, *refs):
    jobs, lo, hi = plan["jobs"], plan["lo"], plan["hi"]
    refs = dict(zip(plan["names"], refs))
    wide, full, sems = refs["wide"], refs["full"], refs["sems"]
    tm, tile, clip = (lax.axis_index(a) for a in ("tm", "tile", "clip"))
    rows, columns, channels = wide.shape[1] - 2, wide.shape[2], full.shape[1]
    cells = float(rows * columns)

    half, core = clip // 2, clip % 2
    copies = []
    for side in range(2):
        for group, names in enumerate(HELD[plan["groups"]]):
            source = refs["w%d" % (side * plan["groups"] + group)]
            high, deep = source.shape[2:]
            for at, (back, dy, dx) in enumerate(names):
                block = (lax.rem(tm + 4 - back, 4) * 2 + (tile ^ dy)) * 2 + (core ^ side)
                place = full.at[
                    :,
                    pl.ds(pl.multiple_of(block * high, high), high),
                    pl.ds(pl.multiple_of((half ^ dx) * deep, 128), deep),
                ]
                piece = source.at[at, pl.ds(lo, hi - lo)]
                copies.append(pltpu.make_async_copy(piece, place, sems.at[len(copies)]))
    slots = plan["slots"]
    count = len(copies)
    early, late = [], []

    def fetch(group, source, place):
        group.append(pltpu.make_async_copy(source, place, sems.at[count + len(early) + len(late)]))
        group[-1].start()

    inner = jnp.where(tile == 0, rows + 1, 0)
    outer = jnp.where(tile == 0, 0, rows + 1)
    fetch(early, refs["vector"], refs["pair"])
    for slot, frame in enumerate(slots):
        ref, at = plan["raw"][frame]
        if len(refs[ref].shape) == 2:
            for r in range(rows):
                line = refs[ref].at[pl.ds(r * columns, columns)]
                fetch(early, line, refs["raw"].at[slot, r + 1])
            near = refs[ref].at[pl.ds(rows * columns, columns + NOTE)]
        else:
            fetch(early, refs[ref].at[at], refs["raw"].at[slot, pl.ds(1, rows)])
            near = refs["other"].at[frame] if frame >= 0 else refs["before"].at[frame + 2]
        fetch(early, near.at[pl.ds(0, columns)], refs["raw"].at[slot, inner])
        fetch(early, near.at[pl.ds(columns, NOTE)], refs["lines"].at[1, slot])
        if frame >= 0:
            lines = refs["note"].at[frame, pl.ds(columns, NOTE)]
            fetch(early, lines, refs["lines"].at[0, slot])
    for copy in copies:
        copy.start()
    for o in jobs:
        if "start" in refs:
            fetch(late, refs["start"].at[o], refs["sum"].at[o])
        if plan["ends"][o] == "final":
            fetch(late, refs["extra"].at[o], refs["rest"].at[o])
    for copy in early:
        copy.wait()

    means, spreads = [[], []], [[], []]
    for slot, frame in enumerate(slots):
        if frame >= 0:
            here = read_note(refs["lines"][0, slot])
        else:
            here = frame_stats(refs["raw"].at[slot, pl.ds(1, rows)])
        there = read_note(refs["lines"][1, slot])
        for side, (mean, spread) in enumerate((here, there)):
            means[side].append(mean)
            spreads[side].append(spread)
    stats = jnp.stack([jnp.concatenate(means[s] + spreads[s], axis=0) for s in range(2)])
    mean_of, scale_of = pool_terms(stats, refs["pair"][0:1], cells)
    for slot in range(len(slots)):
        refs["terms"][slot, 0:1] = mean_of[slot : slot + 1]
        refs["terms"][slot, 1:2] = scale_of[slot : slot + 1] * 0.5
        wide[slot, outer] = jnp.zeros((columns, 3 * channels), BF16)

    column = lax.broadcasted_iota(jnp.int32, (columns, channels), 0)
    halos = sum(frame < 0 for frame in slots)
    shown = rows + 1

    def put(i, carry):
        slot = i // shown
        row = i % shown + jnp.where(tile == 0, 1, 0)
        x = refs["raw"][slot, row].astype(F32)
        half_y = (x - refs["terms"][slot, 0:1]) * refs["terms"][slot, 1:2]
        y = half_y * (1.0 + jnp.tanh(half_y))
        if halos:
            y = jnp.where((slot < halos) & (tm == 0), 0.0, y)
        left = jnp.where(column == 0, 0.0, pltpu.roll(y, 1, 0))
        right = jnp.where(column == columns - 1, 0.0, pltpu.roll(y, columns - 1, 0))
        wide[slot, row, :, :channels] = left.astype(BF16)
        wide[slot, row, :, channels : 2 * channels] = y.astype(BF16)
        wide[slot, row, :, 2 * channels :] = right.astype(BF16)
        return carry

    lax.fori_loop(0, len(slots) * shown, put, 0, unroll=3)

    for copy in copies:
        copy.wait()

    step = BLOCK // columns
    leaving = []
    for o, dfs in jobs.items():
        kind = plan["ends"][o]

        def leave(m, o=o):
            here = pl.ds(m * step, step)
            spot = refs["done_at"].at[o, here]
            place = refs["out"].at[plan["spot"].get(o, o), here]
            return pltpu.make_async_copy(spot, place, refs["done_sem"].at[o * rows + m])

        def block(m, carry, o=o, dfs=dfs, kind=kind, leave=leave):
            here = pl.ds(m * step, step)
            flat = pl.ds(pl.multiple_of(m * BLOCK, BLOCK), BLOCK)
            total = None if "start" in refs else jnp.broadcast_to(
                refs["pair"][1:2], (BLOCK, channels)
            )
            for df in dfs:
                slot = slots.index(o + df - 2)
                for dh in range(3):
                    left = wide[slot, pl.ds(dh + m * step, step)].reshape(BLOCK, 3 * channels)
                    tap = 9 * df + 3 * dh - lo
                    right = jnp.concatenate([full[tap + i] for i in range(3)], axis=1)
                    part = lax.dot_general(left, right, NT, preferred_element_type=F32)
                    total = part if total is None else total + part
            if late and o == list(jobs)[0]:

                @pl.when(m == 0)
                def _():
                    for copy in late:
                        copy.wait()

            if "start" in refs:
                total = total + refs["sum"][o, flat]
            if kind == "partial":
                refs["partial"][o, flat] = total
                return carry
            if kind == "final":
                total = total + refs["rest"][o, here].astype(F32).reshape(BLOCK, channels)
            refs["done_at"][o, here] = total.astype(BF16).reshape(step, columns, channels)
            leave(m).start()
            return carry

        lax.fori_loop(0, rows // step, block, 0)
        if kind == "hidden":
            mean, spread = frame_stats(refs["done_at"].at[o])
            edge = refs["done_at"][o, jnp.where(tile == 0, rows - 1, 0)]
            write_note(refs["new"].at[plan["spot"].get(o, o)], edge, mean, spread)
            if "keep" in refs:
                keep = pltpu.make_async_copy(refs["keep"], refs["new"].at[pl.ds(1, 1)], sems.at[0])
                keep.start()
                keep.wait()
        if kind != "partial":
            leaving += [leave(m) for m in range(rows // step)]
    for copy in leaving:
        copy.wait()


def part_conv(inputs, outputs, jobs, ends, raw, weights, aliases=None, cost=1 << 10, spot={}, **more):
    slots = sorted({o + df - 2 for o, dfs in jobs.items() for df in dfs})
    dfs = sorted({df for group in jobs.values() for df in group})
    lo, hi = 9 * dfs[0], 9 * (dfs[-1] + 1)
    inputs = {**inputs, **{"w%d" % i: w for i, w in enumerate(weights)}}
    _, rows, columns, channels = inputs[next(n for n in ("own", "extra", "own0") if n in inputs)].shape
    plan = dict(spot=spot, groups=len(weights) // 2, jobs=jobs, ends=ends, raw=raw, slots=slots, lo=lo, hi=hi, **more)
    scratch = ["wide", "full", "sems", "raw", "lines", "sum", "rest", "terms", "pair", "done_at", "done_sem"]
    plan["names"] = [*inputs, *outputs, *scratch]
    small = ()
    vmem = pl.BlockSpec(memory_space=pltpu.VMEM)
    anywhere = pl.BlockSpec(memory_space=pl.ANY)
    aliases = aliases or {}
    out_specs = [anywhere if name == "out" else vmem for name in outputs]
    return pl.pallas_call(
        functools.partial(part_kernel, plan),
        out_shape=list(outputs.values()),
        in_specs=[vmem if name in small else anywhere for name in inputs],
        out_specs=out_specs,
        scratch_shapes=[
            pltpu.VMEM((len(slots), rows + 2, columns, 3 * channels), BF16),
            pltpu.VMEM((hi - lo, channels, channels), BF16),
            pltpu.SemaphoreType.DMA((80,)),
            pltpu.VMEM((len(slots), rows + 2, columns, channels), BF16),
            pltpu.VMEM((2, len(slots), NOTE, channels), BF16),
            pltpu.VMEM((2 if "start" in inputs else 1, rows * columns, channels), F32),
            pltpu.VMEM((2, rows, columns, channels), BF16),
            pltpu.VMEM((len(slots), 8, channels), F32),
            pltpu.VMEM((2, channels), F32),
            pltpu.VMEM((2, rows, columns, channels), BF16),
            pltpu.SemaphoreType.DMA((2 * rows,)),
        ],
        input_output_aliases={
            list(inputs).index(source): list(outputs).index(target)
            for source, target in aliases.items()
        },
        cost_estimate=pl.CostEstimate(
            flops=cost,
            bytes_accessed=1 << 10,
            transcendentals=0,
        ),
        name="conv_" + "_".join("%d%s" % (o, "".join(map(str, d))) for o, d in jobs.items()),
    )(*inputs.values())


def along_tm(quarter):
    return [cyclic(quarter, "tm", steps) for steps in (3, 2, 1)][::-1]


def both_cores(arrays):
    return arrays + [swap(a, "clip", 1) for a in arrays]


def hold(*values):
    return lax.optimization_barrier(values)


def shards_fast(
    latents, norm1_gain, conv1_weight, conv1_bias, norm2_gain, conv2_weight, conv2_bias
):
    _, rows, columns, channels = latents.shape
    block = jax.ShapeDtypeStruct(latents.shape, BF16)
    frame = jax.ShapeDtypeStruct((1, rows, columns, channels), BF16)
    note_like = jax.ShapeDtypeStruct((1, columns + NOTE, channels), BF16)
    notes_like = jax.ShapeDtypeStruct((2, columns + NOTE, channels), BF16)
    vector1 = jnp.stack([norm1_gain, conv1_bias])
    vector2 = jnp.stack([norm2_gain, conv2_bias])

    quarter1, quarter2 = own_piece(conv1_weight)[None], own_piece(conv2_weight)[None]
    turned = along_tm(quarter1)
    near1 = swap(quarter1, "clip", 2), swap(quarter1, "tile", 1)
    quarter1_n, latents_n = hold(quarter1, latents)
    notes = notes_of(latents_n)
    other = swap(notes, "tile", 1)
    turned, near1, other, latents_b = hold(turned, near1, other, latents)

    flat = latents_b.reshape(2, rows * columns, channels)
    send1 = jnp.concatenate([flat[1], other[1]])
    send0 = jnp.concatenate([flat[0], other[0]])
    up1 = upward(send1, "tm")
    held1 = jnp.concatenate(turned)
    far1 = swap(held1, "clip", 2), swap(held1, "tile", 1)
    far1, up1, quarter2 = hold(far1, up1, quarter2)

    corners1 = (
        swap(jnp.concatenate([near1[1], far1[1][:1]]), "clip", 2),
        swap(far1[0][1:], "tile", 1),
    )
    weights1 = both_cores([quarter1, held1, *near1, *far1, *corners1])
    turned2 = along_tm(quarter2)
    turned2, send0 = hold(turned2, send0)
    up0 = upward(send0, "tm")
    held2 = jnp.concatenate([quarter2, *turned2])
    weights1, held2 = hold(weights1, held2)
    far2 = swap(held2, "clip", 2), swap(held2, "tile", 1)
    first = dict(note=notes, other=other, vector=vector1, own=latents)
    hidden1, note1 = part_conv(
        {**first, "odd": up1},
        {"out": frame, "new": note_like},
        {1: (0, 1, 2)},
        {1: "hidden"},
        {-1: ("odd", 0), 0: ("own", 0), 1: ("own", 1)},
        weights1,
        cost=1 << 34,
        spot={1: 0},
    )

    high1 = upward(hidden1, "tm")
    far2, up0 = hold(far2, up0)
    corners2 = swap(far2[1][:2], "clip", 2), swap(far2[0][2:], "tile", 1)
    hidden0, notes_h = part_conv(
        {**first, "odd": up1, "even": up0, "keep": note1},
        {"out": frame, "new": notes_like},
        {0: (0, 1, 2)},
        {0: "hidden"},
        {-2: ("even", 0), -1: ("odd", 0), 0: ("own", 0)},
        weights1,
        cost=1 << 34,
    )

    other_h = swap(notes_h, "tile", 1)
    before_h = diagonal(notes_h)
    hidden0_d = hidden0
    high0 = upward(hidden0_d, "tm")
    weights2 = both_cores([held2, *far2, *corners2])
    (out,) = part_conv(
        dict(
            note=notes_h, other=other_h, before=before_h, vector=vector2, own0=hidden0,
            own1=hidden1, odd=high1, even=high0, extra=latents,
        ),
        {"out": block},
        {1: (0, 1, 2), 0: (0, 1, 2)},
        {1: "final", 0: "final"},
        {-2: ("even", 0), -1: ("odd", 0), 0: ("own0", 0), 1: ("own1", 0)},
        weights2,
    )
    return out


def solution(mesh):
    placed = (
        P(("clip", "tm"), "tile", None, None),
        P(),
        P(None, None, ("tm", "tile")),
        P(),
        P(),
        P(None, None, ("tm", "tile")),
        P(),
    )
    sizes = tuple(mesh.shape[a] for a in ("tm", "tile", "clip"))
    return jax.shard_map(
        shards_fast if sizes == (4, 2, 4) else shards,
        mesh=mesh,
        in_specs=placed,
        out_specs=P(("clip", "tm"), "tile", None, None),
        check_vma=False,
    )
```

```python
import functools

import jax
import jax.numpy as jnp
from jax import lax
from jax.experimental import pallas as pl
from jax.experimental.pallas import tpu as pltpu
from jax.sharding import PartitionSpec as P

GROUPS = 32
TAPS = 27
epsilon = 1e-06
F32 = jnp.float32
BF16 = jnp.bfloat16
NT = (((1,), (1,)), ((), ()))


def upward(value, axis, steps=1):
    count = lax.axis_size(axis)
    first, last = (max(0, -steps), min(count, count - steps))
    return lax.ppermute(value, axis, [(source, source + steps) for source in range(first, last)])


def cyclic(value, axis, steps):
    count = lax.axis_size(axis)
    return lax.ppermute(value, axis, [(i, (i + steps) % count) for i in range(count)])


def swap(value, axis, bit):
    count = lax.axis_size(axis)
    return lax.ppermute(value, axis, [(i, i ^ bit) for i in range(count)])


def edge_rows(block):
    tiles = lax.axis_size("tile")
    if tiles == 2:
        mine = jnp.where(lax.axis_index("tile") == 0, block[:, -1:], block[:, :1])
        own = swap(mine, "tile", 1)
        blocks = lax.axis_size("tm")
        pairs = [(t * 2 + y, (t + 1) * 2 + 1 - y) for t in range(blocks - 1) for y in range(2)]
        before = lax.ppermute(mine, ("tm", "tile"), pairs)
        return own, own, before, before
    low = upward(block[:, -1:], "tile", 1)
    high = upward(block[:, :1], "tile", -1)
    return low, high, upward(low, "tm"), upward(high, "tm")


def share_stats(stats):
    if lax.axis_size("tile") == 2:
        both = jnp.stack([stats, swap(stats, "tile", 1)])
    else:
        both = lax.all_gather(stats, "tile", axis=0)
    return both, upward(both, "tm")


def whole_weights(shard):
    whole = lax.all_gather(shard, ("tm", "tile"), axis=2, tiled=True)
    return whole.reshape(-1, whole.shape[2]).T


def channel_stats(rows):
    mean = jnp.sum(rows, axis=0, keepdims=True) / rows.shape[0]
    centered = rows - mean
    return mean, jnp.sum(centered * centered, axis=0, keepdims=True)


def stats_kernel(x_ref, s_ref):
    frames, rows, columns, channels = x_ref.shape
    for f in range(frames):
        mean, spread = channel_stats(x_ref[f].astype(F32).reshape(rows * columns, channels))
        s_ref[f : f + 1] = mean
        s_ref[frames + f : frames + f + 1] = spread


def stats_of(block):
    frames, _, _, channels = block.shape
    return pl.pallas_call(
        stats_kernel,
        out_shape=jax.ShapeDtypeStruct((2 * frames, channels), F32),
        in_specs=[pl.BlockSpec(memory_space=pltpu.VMEM)],
        out_specs=pl.BlockSpec(memory_space=pltpu.VMEM),
        name="stats",
    )(block)


def norm_terms(stats, gain, cells):
    tiles, twice, channels = stats.shape
    frames = twice // 2
    width = channels // GROUPS
    a = lax.broadcasted_iota(jnp.int32, (channels, channels), 0) // width
    b = lax.broadcasted_iota(jnp.int32, (channels, channels), 1) // width
    same = jnp.where(a == b, 1.0, 0.0).astype(F32)
    pool = functools.partial(jnp.dot, precision=lax.Precision.HIGHEST, preferred_element_type=F32)
    mean = pool(jnp.sum(stats[:, :frames], axis=0), same) / (tiles * width)
    off = stats[:, :frames] - mean[None]
    spread = jnp.sum(stats[:, frames:] + cells * (off * off), axis=0)
    var = pool(spread, same) / (tiles * width * cells)
    return mean, lax.rsqrt(var + epsilon) * gain


def pool_terms(stats, gain, cells):
    tiles, twice, channels = stats.shape
    frames = twice // 2
    width = channels // GROUPS
    a = lax.broadcasted_iota(jnp.int32, (channels, channels), 0) // width
    b = lax.broadcasted_iota(jnp.int32, (channels, channels), 1) // width
    same = jnp.where(a == b, 1.0, 0.0).astype(BF16)

    def pool(value):
        parts = jnp.concatenate(parts_of(value), axis=0).astype(BF16)
        sums = jnp.dot(parts, same, preferred_element_type=F32)
        return sums[:frames] + sums[frames : 2 * frames] + sums[2 * frames :]

    mean = pool(jnp.sum(stats[:, :frames], axis=0)) / (tiles * width)
    off = stats[:, :frames] - mean[None]
    spread = jnp.sum(stats[:, frames:] + cells * (off * off), axis=0)
    var = pool(spread) / (tiles * width * cells)
    return mean, lax.rsqrt(var + epsilon) * gain


def conv_kernel(n_weights, residual, *refs):
    own, prev, low_o, high_o, low_p, high_p, st_o, st_p, gain, bias = refs[:10]
    weights = refs[10 : 10 + n_weights]
    if residual:
        extra, out = refs[10 + n_weights : 12 + n_weights]
        wide, full, sems = refs[12 + n_weights :]
    else:
        out, stats_out = refs[10 + n_weights : 12 + n_weights]
        wide, full, sems = refs[12 + n_weights :]
    frames, rows, columns, channels = own.shape
    span = 3 * channels

    copies = [pltpu.make_async_copy(weights[0], full, sems.at[0])]
    for copy in copies:
        copy.start()

    cells = float(rows * columns)
    here = norm_terms(st_o[...], gain[...], cells)
    before = norm_terms(st_p[...], gain[...], cells)
    first_tile = lax.axis_index("tile") == 0
    last_tile = lax.axis_index("tile") == lax.axis_size("tile") - 1
    start = lax.axis_index("tm") == 0
    column = lax.broadcasted_iota(jnp.int32, (columns, channels), 0)

    def put(slot, row, raw, mean, scale, empty):
        half_y = (raw.astype(F32) - mean) * (0.5 * scale)
        y = half_y * (1.0 + jnp.tanh(half_y))
        if empty is not None:
            y = jnp.where(empty, 0.0, y)
        left = jnp.where(column == 0, 0.0, pltpu.roll(y, 1, 0))
        right = jnp.where(column == columns - 1, 0.0, pltpu.roll(y, columns - 1, 0))
        wide[slot, row, :, :channels] = left.astype(BF16)
        wide[slot, row, :, channels : 2 * channels] = y.astype(BF16)
        wide[slot, row, :, 2 * channels :] = right.astype(BF16)

    for f in range(2):
        mean, scale = here[0][f : f + 1], here[1][f : f + 1]

        def body(r, carry, f=f, mean=mean, scale=scale):
            put(2 + f, r + 1, own[f, r], mean, scale, None)
            return carry

        lax.fori_loop(0, rows, body, 0)
        put(2 + f, 0, low_o[f, 0], mean, scale, first_tile)
        put(2 + f, rows + 1, high_o[f, 0], mean, scale, last_tile)
    for f in range(2):
        mean, scale = before[0][f : f + 1], before[1][f : f + 1]

        def body(r, carry, f=f, mean=mean, scale=scale):
            put(f, r + 1, prev[f, r], mean, scale, start)
            return carry

        lax.fori_loop(0, rows, body, 0)
        put(f, 0, low_p[f, 0], mean, scale, start | first_tile)
        put(f, rows + 1, high_p[f, 0], mean, scale, start | last_tile)

    for copy in copies:
        copy.wait()

    def frame(f, carry):
        total = jnp.broadcast_to(bias[...], (rows * columns, channels))
        for df in range(3):
            for dh in range(3):
                left = wide[f + df, dh : dh + rows].reshape(rows * columns, span)
                at = (3 * df + dh) * span
                total = total + lax.dot_general(
                    left, full[:, at : at + span], NT, preferred_element_type=F32
                )
        if residual:
            total = total + extra[f].astype(F32).reshape(rows * columns, channels)
        done = total.astype(BF16)
        out[f] = done.reshape(rows, columns, channels)
        if not residual:
            mean, spread = channel_stats(done.astype(F32))
            stats_out[pl.ds(f, 1)] = mean
            stats_out[pl.ds(frames + f, 1)] = spread
        return carry

    lax.fori_loop(0, frames, frame, 0)


def conv(own, prev, edges, stats, gain, bias, weights, extra=None):
    frames, rows, columns, channels = own.shape
    vmem = pl.BlockSpec(memory_space=pltpu.VMEM)
    shapes = [jax.ShapeDtypeStruct(own.shape, BF16)]
    args = [own, prev, *edges, *stats, gain[None], bias[None], *weights]
    specs = [vmem] * 10 + [pl.BlockSpec(memory_space=pl.ANY)] * len(weights)
    if extra is None:
        shapes.append(jax.ShapeDtypeStruct((2 * frames, channels), F32))
    else:
        args.append(extra)
        specs.append(vmem)
    flops = 2 * frames * rows * columns * channels * channels * TAPS
    return pl.pallas_call(
        functools.partial(conv_kernel, len(weights), extra is not None),
        out_shape=shapes,
        in_specs=specs,
        out_specs=[vmem] * len(shapes),
        scratch_shapes=[
            pltpu.VMEM((4, rows + 2, columns, 3 * channels), BF16),
            pltpu.VMEM((channels, TAPS * channels), BF16),
            pltpu.SemaphoreType.DMA((1,)),
        ],
        cost_estimate=pl.CostEstimate(flops=flops, bytes_accessed=9 << 20, transcendentals=1 << 20),
        name="conv",
    )(*args)


def shards(latents, norm1_gain, conv1_weight, conv1_bias, norm2_gain, conv2_weight, conv2_bias):
    weights1 = [whole_weights(conv1_weight)]
    prev = upward(latents, "tm")
    edges = edge_rows(latents)
    stats = share_stats(stats_of(latents))
    hidden, sums = conv(latents, prev, edges, stats, norm1_gain, conv1_bias, weights1)
    weights2 = [whole_weights(conv2_weight)]
    prev = upward(hidden, "tm")
    edges = edge_rows(hidden)
    stats = share_stats(sums)
    return conv(hidden, prev, edges, stats, norm2_gain, conv2_bias, weights2, latents)[0]


HELD = {
    8: (
        ((0, 0, 0),),
        ((1, 0, 0), (2, 0, 0), (3, 0, 0)),
        ((0, 0, 1),),
        ((0, 1, 0),),
        ((1, 0, 1), (2, 0, 1), (3, 0, 1)),
        ((1, 1, 0), (2, 1, 0), (3, 1, 0)),
        ((0, 1, 1), (1, 1, 1)),
        ((2, 1, 1), (3, 1, 1)),
    ),
    5: (
        ((0, 0, 0), (1, 0, 0), (2, 0, 0), (3, 0, 0)),
        ((0, 0, 1), (1, 0, 1), (2, 0, 1), (3, 0, 1)),
        ((0, 1, 0), (1, 1, 0), (2, 1, 0), (3, 1, 0)),
        ((0, 1, 1), (1, 1, 1)),
        ((2, 1, 1), (3, 1, 1)),
    ),
}
BLOCK = 512
NOTE = 16


def own_piece(shard):
    turned = jnp.swapaxes(shard, 1, 2)
    taps, outs, depth = turned.shape
    clip = lax.axis_index("clip")
    start = (0, (clip % 2) * (outs // 2), (clip // 2) * (depth // 2))
    return lax.dynamic_slice(turned, start, (taps, outs // 2, depth // 2))


def diagonal(note):
    blocks = lax.axis_size("tm")
    pairs = [(t * 2 + y, (t + 1) * 2 + 1 - y) for t in range(blocks - 1) for y in range(2)]
    return lax.ppermute(note, ("tm", "tile"), pairs)


def parts_of(value):
    first = value.astype(BF16).astype(F32)
    second = (value - first).astype(BF16).astype(F32)
    return [first, second, value - first - second]


def write_note(note, edge, mean, spread):
    columns, channels = edge.shape
    note[:columns] = edge
    lines = parts_of(mean) + parts_of(spread)
    lines.append(jnp.zeros((NOTE - 6, channels), F32))
    note[columns:] = jnp.concatenate(lines, axis=0).astype(BF16)


def read_note(lines):
    lines = lines.astype(F32)
    mean = lines[0:1] + lines[1:2] + lines[2:3]
    spread = lines[3:4] + lines[4:5] + lines[5:6]
    return mean, spread


def frame_stats(frame):
    rows, columns, channels = frame.shape

    def total(of):
        def body(r, carry):
            value = of(frame[r].astype(F32))
            return carry + jnp.sum(value.reshape(columns // 8, 8, channels), axis=0)

        lines = lax.fori_loop(0, rows, body, jnp.zeros((8, channels), F32), unroll=8)
        return jnp.sum(lines, axis=0, keepdims=True)

    mean = total(lambda x: x) / (rows * columns)

    def squared(x):
        centered = x - mean
        return centered * centered

    return mean, total(squared)


def notes_kernel(x_ref, note_ref):
    frames, rows, columns, channels = x_ref.shape
    at = jnp.where(lax.axis_index("tile") == 0, rows - 1, 0)
    for f in range(frames):
        mean, spread = frame_stats(x_ref.at[f])
        write_note(note_ref.at[f], x_ref[f, at], mean, spread)


def notes_of(block):
    frames, _, columns, channels = block.shape
    return pl.pallas_call(
        notes_kernel,
        out_shape=jax.ShapeDtypeStruct((frames, columns + NOTE, channels), BF16),
        in_specs=[pl.BlockSpec(memory_space=pltpu.VMEM)],
        out_specs=pl.BlockSpec(memory_space=pltpu.VMEM),
        cost_estimate=pl.CostEstimate(flops=1 << 34, bytes_accessed=1 << 10, transcendentals=0),
        name="notes",
    )(block)


def part_kernel(plan, *refs):
    jobs, lo, hi = plan["jobs"], plan["lo"], plan["hi"]
    refs = dict(zip(plan["names"], refs))
    wide, full, sems = refs["wide"], refs["full"], refs["sems"]
    tm, tile, clip = (lax.axis_index(a) for a in ("tm", "tile", "clip"))
    rows, columns, channels = wide.shape[1] - 2, wide.shape[2], full.shape[1]
    cells = float(rows * columns)

    half, core = clip // 2, clip % 2
    copies = []
    for side in range(2):
        for group, names in enumerate(HELD[plan["groups"]]):
            source = refs["w%d" % (side * plan["groups"] + group)]
            high, deep = source.shape[2:]
            for at, (back, dy, dx) in enumerate(names):
                block = (lax.rem(tm + 4 - back, 4) * 2 + (tile ^ dy)) * 2 + (core ^ side)
                place = full.at[
                    :,
                    pl.ds(pl.multiple_of(block * high, high), high),
                    pl.ds(pl.multiple_of((half ^ dx) * deep, 128), deep),
                ]
                piece = source.at[at, pl.ds(lo, hi - lo)]
                copies.append(pltpu.make_async_copy(piece, place, sems.at[len(copies)]))
    slots = plan["slots"]
    count = len(copies)
    early, late = [], []

    def fetch(group, source, place):
        group.append(pltpu.make_async_copy(source, place, sems.at[count + len(early) + len(late)]))
        group[-1].start()

    inner = jnp.where(tile == 0, rows + 1, 0)
    outer = jnp.where(tile == 0, 0, rows + 1)
    fetch(early, refs["vector"], refs["pair"])
    for slot, frame in enumerate(slots):
        ref, at = plan["raw"][frame]
        if len(refs[ref].shape) == 2:
            for r in range(rows):
                line = refs[ref].at[pl.ds(r * columns, columns)]
                fetch(early, line, refs["raw"].at[slot, r + 1])
            near = refs[ref].at[pl.ds(rows * columns, columns + NOTE)]
        else:
            fetch(early, refs[ref].at[at], refs["raw"].at[slot, pl.ds(1, rows)])
            near = refs["other"].at[frame] if frame >= 0 else refs["before"].at[frame + 2]
        fetch(early, near.at[pl.ds(0, columns)], refs["raw"].at[slot, inner])
        fetch(early, near.at[pl.ds(columns, NOTE)], refs["lines"].at[1, slot])
        if frame >= 0:
            lines = refs["note"].at[frame, pl.ds(columns, NOTE)]
            fetch(early, lines, refs["lines"].at[0, slot])
    for copy in copies:
        copy.start()
    for o in jobs:
        if "start" in refs:
            fetch(late, refs["start"].at[o], refs["sum"].at[o])
        if plan["ends"][o] == "final":
            fetch(late, refs["extra"].at[o], refs["rest"].at[o])
    for copy in early:
        copy.wait()

    means, spreads = [[], []], [[], []]
    for slot, frame in enumerate(slots):
        if frame >= 0:
            here = read_note(refs["lines"][0, slot])
        else:
            here = frame_stats(refs["raw"].at[slot, pl.ds(1, rows)])
        there = read_note(refs["lines"][1, slot])
        for side, (mean, spread) in enumerate((here, there)):
            means[side].append(mean)
            spreads[side].append(spread)
    stats = jnp.stack([jnp.concatenate(means[s] + spreads[s], axis=0) for s in range(2)])
    mean_of, scale_of = pool_terms(stats, refs["pair"][0:1], cells)
    for slot in range(len(slots)):
        refs["terms"][slot, 0:1] = mean_of[slot : slot + 1]
        refs["terms"][slot, 1:2] = scale_of[slot : slot + 1] * 0.5
        wide[slot, outer] = jnp.zeros((columns, 3 * channels), BF16)

    column = lax.broadcasted_iota(jnp.int32, (columns, channels), 0)
    halos = sum(frame < 0 for frame in slots)
    shown = rows + 1

    def put(i, carry):
        slot = i // shown
        row = i % shown + jnp.where(tile == 0, 1, 0)
        x = refs["raw"][slot, row].astype(F32)
        half_y = (x - refs["terms"][slot, 0:1]) * refs["terms"][slot, 1:2]
        y = half_y * (1.0 + jnp.tanh(half_y))
        if halos:
            y = jnp.where((slot < halos) & (tm == 0), 0.0, y)
        left = jnp.where(column == 0, 0.0, pltpu.roll(y, 1, 0))
        right = jnp.where(column == columns - 1, 0.0, pltpu.roll(y, columns - 1, 0))
        wide[slot, row, :, :channels] = left.astype(BF16)
        wide[slot, row, :, channels : 2 * channels] = y.astype(BF16)
        wide[slot, row, :, 2 * channels :] = right.astype(BF16)
        return carry

    lax.fori_loop(0, len(slots) * shown, put, 0, unroll=9)

    for copy in copies:
        copy.wait()

    size = BLOCK * 2 // len(jobs)
    step = size // columns
    leaving = []
    for o, dfs in jobs.items():
        kind = plan["ends"][o]

        def leave(m, o=o):
            here = pl.ds(m * step, step)
            spot = refs["done_at"].at[o, here]
            place = refs["out"].at[plan["spot"].get(o, o), here]
            return pltpu.make_async_copy(spot, place, refs["done_sem"].at[o * rows + m])

        def block(m, carry, o=o, dfs=dfs, kind=kind, leave=leave):
            here = pl.ds(m * step, step)
            flat = pl.ds(pl.multiple_of(m * size, size), size)
            total = None if "start" in refs else jnp.broadcast_to(
                refs["pair"][1:2], (size, channels)
            )
            for df in dfs:
                slot = slots.index(o + df - 2)
                for dh in range(3):
                    left = wide[slot, pl.ds(dh + m * step, step)].reshape(size, 3 * channels)
                    tap = 9 * df + 3 * dh - lo
                    right = jnp.concatenate([full[tap + i] for i in range(3)], axis=1)
                    part = lax.dot_general(left, right, NT, preferred_element_type=F32)
                    total = part if total is None else total + part
            if late and o == list(jobs)[0]:

                @pl.when(m == 0)
                def _():
                    for copy in late:
                        copy.wait()

            if "start" in refs:
                total = total + refs["sum"][o, flat]
            if kind == "partial":
                refs["partial"][o, flat] = total
                return carry
            if kind == "final":
                total = total + refs["rest"][o, here].astype(F32).reshape(size, channels)
            refs["done_at"][o, here] = total.astype(BF16).reshape(step, columns, channels)
            leave(m).start()
            return carry

        lax.fori_loop(0, rows // step, block, 0)
        if kind == "hidden":
            mean, spread = frame_stats(refs["done_at"].at[o])
            edge = refs["done_at"][o, jnp.where(tile == 0, rows - 1, 0)]
            write_note(refs["new"].at[plan["spot"].get(o, o)], edge, mean, spread)
            if "keep" in refs:
                keep = pltpu.make_async_copy(refs["keep"], refs["new"].at[pl.ds(1, 1)], sems.at[0])
                keep.start()
                keep.wait()
        if kind != "partial":
            leaving += [leave(m) for m in range(rows // step)]
    for copy in leaving:
        copy.wait()


def part_conv(inputs, outputs, jobs, ends, raw, weights, aliases=None, cost=1 << 10, spot={}, **more):
    slots = sorted({o + df - 2 for o, dfs in jobs.items() for df in dfs})
    dfs = sorted({df for group in jobs.values() for df in group})
    lo, hi = 9 * dfs[0], 9 * (dfs[-1] + 1)
    inputs = {**inputs, **{"w%d" % i: w for i, w in enumerate(weights)}}
    _, rows, columns, channels = inputs[next(n for n in ("own", "extra", "own0") if n in inputs)].shape
    plan = dict(spot=spot, groups=len(weights) // 2, jobs=jobs, ends=ends, raw=raw, slots=slots, lo=lo, hi=hi, **more)
    scratch = ["wide", "full", "sems", "raw", "lines", "sum", "rest", "terms", "pair", "done_at", "done_sem"]
    plan["names"] = [*inputs, *outputs, *scratch]
    small = ()
    vmem = pl.BlockSpec(memory_space=pltpu.VMEM)
    anywhere = pl.BlockSpec(memory_space=pl.ANY)
    aliases = aliases or {}
    out_specs = [anywhere if name == "out" else vmem for name in outputs]
    return pl.pallas_call(
        functools.partial(part_kernel, plan),
        out_shape=list(outputs.values()),
        in_specs=[vmem if name in small else anywhere for name in inputs],
        out_specs=out_specs,
        scratch_shapes=[
            pltpu.VMEM((len(slots), rows + 2, columns, 3 * channels), BF16),
            pltpu.VMEM((hi - lo, channels, channels), BF16),
            pltpu.SemaphoreType.DMA((80,)),
            pltpu.VMEM((len(slots), rows + 2, columns, channels), BF16),
            pltpu.VMEM((2, len(slots), NOTE, channels), BF16),
            pltpu.VMEM((2 if "start" in inputs else 1, rows * columns, channels), F32),
            pltpu.VMEM((2, rows, columns, channels), BF16),
            pltpu.VMEM((len(slots), 8, channels), F32),
            pltpu.VMEM((2, channels), F32),
            pltpu.VMEM((2, rows, columns, channels), BF16),
            pltpu.SemaphoreType.DMA((2 * rows,)),
        ],
        input_output_aliases={
            list(inputs).index(source): list(outputs).index(target)
            for source, target in aliases.items()
        },
        cost_estimate=pl.CostEstimate(
            flops=cost,
            bytes_accessed=1 << 10,
            transcendentals=0,
        ),
        name="conv_" + "_".join("%d%s" % (o, "".join(map(str, d))) for o, d in jobs.items()),
    )(*inputs.values())


def along_tm(quarter):
    return [cyclic(quarter, "tm", steps) for steps in (3, 2, 1)][::-1]


def both_cores(arrays):
    return arrays + [swap(a, "clip", 1) for a in arrays]


def hold(*values):
    return lax.optimization_barrier(values)


def shards_fast(
    latents, norm1_gain, conv1_weight, conv1_bias, norm2_gain, conv2_weight, conv2_bias
):
    _, rows, columns, channels = latents.shape
    block = jax.ShapeDtypeStruct(latents.shape, BF16)
    frame = jax.ShapeDtypeStruct((1, rows, columns, channels), BF16)
    note_like = jax.ShapeDtypeStruct((1, columns + NOTE, channels), BF16)
    notes_like = jax.ShapeDtypeStruct((2, columns + NOTE, channels), BF16)
    vector1 = jnp.stack([norm1_gain, conv1_bias])
    vector2 = jnp.stack([norm2_gain, conv2_bias])

    quarter1, quarter2 = own_piece(conv1_weight)[None], own_piece(conv2_weight)[None]
    turned = along_tm(quarter1)
    near1 = swap(quarter1, "clip", 2), swap(quarter1, "tile", 1)
    quarter1_n, latents_n = hold(quarter1, latents)
    notes = notes_of(latents_n)
    other = swap(notes, "tile", 1)
    turned, near1, other, latents_b = hold(turned, near1, other, latents)

    flat = latents_b.reshape(2, rows * columns, channels)
    send1 = jnp.concatenate([flat[1], other[1]])
    send0 = jnp.concatenate([flat[0], other[0]])
    up1 = upward(send1, "tm")
    held1 = jnp.concatenate(turned)
    far1 = swap(held1, "clip", 2), swap(held1, "tile", 1)
    far1, up1, quarter2 = hold(far1, up1, quarter2)

    corners1 = (
        swap(jnp.concatenate([near1[1], far1[1][:1]]), "clip", 2),
        swap(far1[0][1:], "tile", 1),
    )
    weights1 = both_cores([quarter1, held1, *near1, *far1, *corners1])
    turned2 = along_tm(quarter2)
    turned2, send0 = hold(turned2, send0)
    up0 = upward(send0, "tm")
    held2 = jnp.concatenate([quarter2, *turned2])
    weights1, held2 = hold(weights1, held2)
    far2 = swap(held2, "clip", 2), swap(held2, "tile", 1)
    first = dict(note=notes, other=other, vector=vector1, own=latents)
    hidden1, note1 = part_conv(
        {**first, "odd": up1},
        {"out": frame, "new": note_like},
        {1: (0, 1, 2)},
        {1: "hidden"},
        {-1: ("odd", 0), 0: ("own", 0), 1: ("own", 1)},
        weights1,
        cost=1 << 34,
        spot={1: 0},
    )

    high1 = upward(hidden1, "tm")
    far2, up0 = hold(far2, up0)
    corners2 = swap(far2[1][:2], "clip", 2), swap(far2[0][2:], "tile", 1)
    hidden0, notes_h = part_conv(
        {**first, "odd": up1, "even": up0, "keep": note1},
        {"out": frame, "new": notes_like},
        {0: (0, 1, 2)},
        {0: "hidden"},
        {-2: ("even", 0), -1: ("odd", 0), 0: ("own", 0)},
        weights1,
        cost=1 << 34,
    )

    other_h = swap(notes_h, "tile", 1)
    before_h = diagonal(notes_h)
    hidden0_d = hidden0
    high0 = upward(hidden0_d, "tm")
    weights2 = both_cores([held2, *far2, *corners2])
    (out,) = part_conv(
        dict(
            note=notes_h, other=other_h, before=before_h, vector=vector2, own0=hidden0,
            own1=hidden1, odd=high1, even=high0, extra=latents,
        ),
        {"out": block},
        {1: (0, 1, 2), 0: (0, 1, 2)},
        {1: "final", 0: "final"},
        {-2: ("even", 0), -1: ("odd", 0), 0: ("own0", 0), 1: ("own1", 0)},
        weights2,
    )
    return out


def solution(mesh):
    placed = (
        P(("clip", "tm"), "tile", None, None),
        P(),
        P(None, None, ("tm", "tile")),
        P(),
        P(),
        P(None, None, ("tm", "tile")),
        P(),
    )
    sizes = tuple(mesh.shape[a] for a in ("tm", "tile", "clip"))
    return jax.shard_map(
        shards_fast if sizes == (4, 2, 4) else shards,
        mesh=mesh,
        in_specs=placed,
        out_specs=P(("clip", "tm"), "tile", None, None),
        check_vma=False,
    )
```
